32 devices in a mesh: section: 2 (over y), expert: 4 (over z), dp: 4 (over x, core).
Axes of the slice: x: 2, y: 2, z: 4, core: 2. Of those that a mesh axis runs over, the one named last changes fastest.
Arguments:
- residual: bfloat16 [4096, 2048], P(('section', 'expert', 'dp')), may hold values from -12 to 12
- queries: bfloat16 [4096, 1024], P(('section', 'expert', 'dp')), may hold values from -6 to 6
- attn_keys: bfloat16 [4096, 1024], P(('section', 'expert', 'dp')), may hold values from -6 to 6
- attn_values: bfloat16 [4096, 1024], P(('section', 'expert', 'dp')), may hold values from -6 to 6
- out_weight: bfloat16 [1024, 2048], P('expert'), may hold values from -0.1875 to 0.1875
- norm_gain: float32 [2048], replicated, may hold values from 0.25 to 1.75
- gate_weight: bfloat16 [4, 2048, 4096], P('expert', None, 'dp'), may hold values from -0.125 to 0.125
- up_weight: bfloat16 [4, 2048, 4096], P('expert', None, 'dp'), may hold values from -0.125 to 0.125
- down_weight: bfloat16 [4, 4096, 2048], P('expert', 'dp'), may hold values from -0.09375 to 0.09375
- expert_ids: int32 [4096, 1], P(('section', 'expert', 'dp')), may hold values from 0 to 3; in each aligned block of 128 rows (0 to 127, 128 to 255, ...) at most 64 rows name the same one
- out_grad: bfloat16 [4096, 2048], P(('section', 'expert', 'dp')), may hold values from -6 to 6
Outputs:
- layer_out: bfloat16 [4096, 2048], P(('section', 'expert', 'dp'))
- resid_grad: bfloat16 [4096, 2048], P(('section', 'expert', 'dp'))
- query_grad: bfloat16 [4096, 1024], P(('section', 'expert', 'dp'))
- key_grad: bfloat16 [4096, 1024], P(('section', 'expert', 'dp'))
- value_grad: bfloat16 [4096, 1024], P(('section', 'expert', 'dp'))
- weight_grad: float32 [1024, 2048], P('expert')
The draws below stay inside these ranges and needn't reach their ends.
Inputs may be any that keep to these rules, and one draw needn't show every extreme that they name: `expert_ids`: no expert is named by more than 64 of the 128 rows of one device (an aligned block); in every draw some block names one expert exactly 64 times.
All inputs are finite; a program needn't handle non-finite values.
Results may differ from the reference program's by a relative error of at most 0.023.
Values may be sent and summed in bfloat16 or wider, within the bound.
A program may use at most 128 MiB of HBM per device.

```python
import math
import jax
import jax.numpy as jnp
import numpy as np
from jax import lax

D = 2048
HEADS = 8
HEAD = 128
A = 1024
FF = 4096
EXPERTS = 4
TOK_DEV = 128
CAP = 64
LEN = 512
SEQS = 8
TOKENS = 4096
N_DP = 4


def query_key_pair(key):
    base_query = jnp.clip(jax.random.normal(jax.random.fold_in(key, 71), (TOKENS, A), jnp.float32) * 1.3, -6.0, 6.0)
    base_key = jnp.clip(jax.random.normal(jax.random.fold_in(key, 72), (TOKENS, A), jnp.float32) * 1.3, -6.0, 6.0)
    return (base_query, base_key)


def draw_queries(key, part):
    return query_key_pair(key)[0].astype(jnp.bfloat16)


def draw_attn_keys(key, part):
    return query_key_pair(key)[1].astype(jnp.bfloat16)


def draw_residual(key, part):
    base_draw = jax.random.normal(jax.random.fold_in(key, 81), (TOKENS, D), jnp.float32)
    row_scale = jnp.exp(jax.random.uniform(jax.random.fold_in(key, 82), (TOKENS, 1), jnp.float32, -0.7, 0.7))
    column_scale = jnp.exp(jax.random.uniform(jax.random.fold_in(key, 83), (1, D), jnp.float32, -0.7, 0.7))
    return jnp.clip(base_draw * row_scale * column_scale, -12.0, 12.0).astype(jnp.bfloat16)


def shard_levels(stream_key, shape, cuts, least, top_value):
    gain = 1.0
    for dim, shards_of in cuts:
        heights = jax.random.uniform(jax.random.fold_in(jax.random.fold_in(stream_key, 6), dim), (shards_of,), jnp.float32, least / len(cuts), top_value / len(cuts))
        gain = gain * jnp.repeat(jnp.exp(heights), shape[dim] // shards_of).reshape((-1,) + (1,) * (len(shape) - 1 - dim))
    return gain


def routed_block(rng, own, number, rows, amount, top, most, slope):
    ranking = jax.random.permutation(rng, amount)
    crowded, ordinary = portions_of(amount, rows * top, most, slope, True), portions_of(amount, rows * top, most, slope, False)
    places = jnp.arange(amount)

    def named(tallies, rotation):
        used = int((tallies > 0).sum())
        fixed = max(1, used // 4)
        moved = fixed + (places - fixed + rotation * (used - fixed)) % max(1, amount - fixed)
        return jnp.zeros((amount,), jnp.int32).at[ranking[jnp.where(places < fixed, places, moved)]].set(jnp.asarray(tallies, jnp.int32))

    tallies = jnp.where(number % 4 == 0, named(crowded, number // 4), named(ordinary, number - number // 4 - 1))
    mixed = jax.random.permutation(jax.random.fold_in(own, 3), amount)
    source_of, sink = mixed[0:amount // 2 * 2:2], mixed[1:amount // 2 * 2:2]
    margin = jnp.minimum(tallies[source_of] - 1, most - tallies[sink]) // 2
    margin = jnp.where((source_of == ranking[0]) | (sink == ranking[0]) | (tallies[sink] == 0), 0, jnp.maximum(margin, 0))
    moved = jax.random.randint(jax.random.fold_in(own, 4), (amount // 2,), 0, 1 << 20) % (margin + 1)
    tallies = tallies.at[source_of].add(-moved).at[sink].add(moved)
    members = jnp.searchsorted(jnp.cumsum(tallies), jnp.arange(rows * top), side="right").astype(jnp.int32)
    table = members.reshape(top, rows).T
    table = table[jax.random.permutation(jax.random.fold_in(own, 1), rows)]
    rotation = jax.random.randint(jax.random.fold_in(own, 2), (rows, 1), 0, top)
    return jnp.take_along_axis(table, (jnp.arange(top)[None, :] + rotation) % top, axis=1)


def portions_of(count, total, limit, skew, full):
    weights = [(1 << 20) // math.isqrt(rank ** skew) + 1 for rank in range(1, count + 1)]
    largest = limit if full else min(limit, max(-(-total // count), total * weights[0] // sum(weights)))
    least = 1 if total - largest >= count - 1 else 0
    counts, surplus = [largest] + [least] * (count - 1), total - largest - least * (count - 1)
    while surplus > 0:
        movable = [i for i in range(1, count) if counts[i] < largest] or [i for i in range(1, count) if counts[i] < limit]
        whole, left = sum([weights[i] for i in movable]), surplus
        for i in movable:
            addition = min(limit - counts[i], max(1, left * weights[i] // whole), surplus)
            counts[i] = counts[i] + addition
            surplus = surplus - addition
    return np.array(counts)


def bell_draw(stream_key, dims, scale, most, shards=(), kind=jnp.bfloat16):
    factor_of = shard_levels(stream_key, dims, shards, -0.22, 0.18) if shards else 1.0
    values = jax.random.normal(stream_key, dims, jnp.float32) * scale * factor_of
    return jnp.minimum(jnp.maximum(values, -most), most).astype(kind)


def setup_inputs(seed: int = 0) -> dict:
    seeds = jax.random.split(jax.random.key(seed), 12)
    residual = draw_residual(jax.random.fold_in(seeds[11], 71), 0)
    queries = draw_queries(jax.random.fold_in(seeds[11], 71), 0)
    attn_keys = draw_attn_keys(jax.random.fold_in(seeds[11], 71), 0)
    attn_values = bell_draw(seeds[3], (TOKENS, A), 1.0, 6.0, ((0, 32),))
    out_weight = bell_draw(seeds[4], (A, D), A ** -0.5, 0.1875, ((0, 4),))
    norm_gain = jnp.clip(1.0 + 0.15 * jax.random.normal(seeds[5], (D,), jnp.float32), 0.25, 1.75)
    gate_weight = bell_draw(seeds[6], (EXPERTS, D, FF), D ** -0.5, 0.125, ((0, 4), (2, 4)))
    up_weight = bell_draw(seeds[7], (EXPERTS, D, FF), D ** -0.5, 0.125, ((0, 4), (2, 4)))
    down_weight = bell_draw(seeds[8], (EXPERTS, FF, D), FF ** -0.5, 0.09375, ((0, 4), (1, 4)))
    expert_ids_keys = jax.random.split(jax.random.fold_in(seeds[9], 1), TOKENS // TOK_DEV)
    expert_ids_turns = jax.random.permutation(jax.random.fold_in(seeds[9], 3), TOKENS // TOK_DEV)
    expert_ids = jax.vmap(lambda own, number: routed_block(jax.random.fold_in(seeds[9], 2), own, number, TOK_DEV, EXPERTS, 1, CAP, 2))(expert_ids_keys, expert_ids_turns).reshape((TOKENS, 1))
    out_grad = bell_draw(seeds[10], (TOKENS, D), 1.0, 6.0, ((0, 32),))
    return {"residual": residual, "queries": queries, "attn_keys": attn_keys, "attn_values": attn_values, "out_weight": out_weight, "norm_gain": norm_gain, "gate_weight": gate_weight, "up_weight": up_weight, "down_weight": down_weight, "expert_ids": expert_ids, "out_grad": out_grad}


epsilon = 1e-06

def low_copy(values):
    return lax.optimization_barrier(values.astype(jnp.bfloat16)).astype(jnp.float32)

def seq_probs(query_block, key_block):
    query_heads = query_block.reshape(LEN, HEADS, HEAD).astype(jnp.float32)
    key_heads = key_block.reshape(LEN, HEADS, HEAD).astype(jnp.float32)
    scores = jnp.einsum('qhd,khd->hqk', query_heads, key_heads) * (1.0 / math.sqrt(HEAD))
    row_peak = lax.optimization_barrier(jnp.max(scores, axis=-1, keepdims=True))
    exp_scores = jnp.exp(scores - row_peak)
    return exp_scores / lax.optimization_barrier(jnp.sum(exp_scores, axis=-1, keepdims=True))

def seq_forward(operands):
    query_block, key_block, value_block = operands
    attn_probs = seq_probs(query_block, key_block)
    value_heads = value_block.reshape(LEN, HEADS, HEAD).astype(jnp.float32)
    mixed_rows = jnp.einsum('hqk,khd->qhd', low_copy(attn_probs), value_heads)
    return mixed_rows.reshape(LEN, A).astype(jnp.bfloat16)

def seq_backward(operands):
    query_block, key_block, value_block, grad_block = operands
    attn_probs = seq_probs(query_block, key_block)
    probs_low = low_copy(attn_probs)
    inv_root = 1.0 / math.sqrt(HEAD)
    query_heads = query_block.reshape(LEN, HEADS, HEAD).astype(jnp.float32)
    key_heads = key_block.reshape(LEN, HEADS, HEAD).astype(jnp.float32)
    value_heads = value_block.reshape(LEN, HEADS, HEAD).astype(jnp.float32)
    grad_heads = grad_block.reshape(LEN, HEADS, HEAD).astype(jnp.float32)
    grad_probs = jnp.einsum('qhd,khd->hqk', grad_heads, value_heads)
    row_delta = lax.optimization_barrier(jnp.sum(attn_probs * grad_probs, axis=-1, keepdims=True))
    grad_scores = low_copy(attn_probs * (grad_probs - row_delta))
    query_grad = (jnp.einsum('hqk,khd->qhd', grad_scores, key_heads) * inv_root).reshape(LEN, A)
    key_grad = (jnp.einsum('hqk,qhd->khd', grad_scores, query_heads) * inv_root).reshape(LEN, A)
    value_grad = jnp.einsum('hqk,qhd->khd', probs_low, grad_heads).reshape(LEN, A)
    return (query_grad.astype(jnp.bfloat16), key_grad.astype(jnp.bfloat16), value_grad.astype(jnp.bfloat16))

def expert_forward(operands):
    row_block, gate_local, up_local, down_local = operands
    gate_pre = jnp.dot(row_block, gate_local, preferred_element_type=jnp.float32)
    up_pre = jnp.dot(row_block, up_local, preferred_element_type=jnp.float32)
    activated = (jax.nn.silu(gate_pre) * up_pre).astype(jnp.bfloat16)
    block_width = FF // N_DP
    running = jnp.zeros((row_block.shape[0], D), jnp.float32)
    for quarter in range(N_DP):
        lower_edge = quarter * block_width
        piece_sum = jnp.dot(activated[:, lower_edge:lower_edge + block_width], down_local[lower_edge:lower_edge + block_width], preferred_element_type=jnp.float32)
        running = running + low_copy(piece_sum)
    return running.astype(jnp.bfloat16)

def expert_backward(operands):
    row_block, grad_block, gate_local, up_local, down_local = operands
    gate_pre = jnp.dot(row_block, gate_local, preferred_element_type=jnp.float32)
    up_pre = jnp.dot(row_block, up_local, preferred_element_type=jnp.float32)
    sigmoid_gate = jax.nn.sigmoid(gate_pre)
    grad_act = lax.dot_general(grad_block, down_local, (((1,), (1,)), ((), ())), preferred_element_type=jnp.float32)
    grad_gate = (grad_act * up_pre * sigmoid_gate * (1.0 + gate_pre * (1.0 - sigmoid_gate))).astype(jnp.bfloat16)
    grad_up = (grad_act * jax.nn.silu(gate_pre)).astype(jnp.bfloat16)
    block_width = FF // N_DP
    running = jnp.zeros((row_block.shape[0], D), jnp.float32)
    for quarter in range(N_DP):
        lower_edge = quarter * block_width
        upper_edge = lower_edge + block_width
        piece_sum = lax.dot_general(grad_gate[:, lower_edge:upper_edge], gate_local[:, lower_edge:upper_edge], (((1,), (1,)), ((), ())), preferred_element_type=jnp.float32)
        piece_sum = piece_sum + lax.dot_general(grad_up[:, lower_edge:upper_edge], up_local[:, lower_edge:upper_edge], (((1,), (1,)), ((), ())), preferred_element_type=jnp.float32)
        running = running + low_copy(piece_sum)
    return running.astype(jnp.bfloat16)

def reference(residual, queries, attn_keys, attn_values, out_weight, norm_gain, gate_weight, up_weight, down_weight, expert_ids, out_grad):
    tiled = (SEQS, LEN, A)
    attended = lax.map(seq_forward, (queries.reshape(tiled), attn_keys.reshape(tiled), attn_values.reshape(tiled))).reshape(TOKENS, A)
    hidden = residual.astype(jnp.float32) + jnp.dot(attended, out_weight, preferred_element_type=jnp.float32)
    inv_rms = lax.rsqrt(lax.optimization_barrier(jnp.mean(hidden * hidden, axis=-1, keepdims=True)) + epsilon)
    unit_rows = hidden * inv_rms
    normed = (unit_rows * norm_gain).astype(jnp.bfloat16)
    expert_of = expert_ids[:, 0].astype(jnp.int32)
    onehot = (expert_of[:, None] == jnp.arange(EXPERTS, dtype=jnp.int32)[None, :]).astype(jnp.int32)
    per_device = onehot.reshape(-1, TOK_DEV, EXPERTS)
    before = jnp.cumsum(per_device, axis=1) - per_device
    rank_index = lax.optimization_barrier(jnp.sum(before * per_device, axis=-1)).reshape(-1)
    device_of = jnp.arange(TOKENS, dtype=jnp.int32) // TOK_DEV
    position = (device_of * CAP + rank_index).astype(jnp.int32)
    slots_all = TOKENS // TOK_DEV * CAP
    empty_buckets = jnp.zeros((EXPERTS, slots_all, D), jnp.bfloat16)
    buckets = empty_buckets.at[expert_of, position].set(normed)
    expert_rows = lax.map(expert_forward, (buckets, gate_weight, up_weight, down_weight))
    expert_back = expert_rows[expert_of, position]
    layer_out = (hidden + expert_back.astype(jnp.float32)).astype(jnp.bfloat16)
    grad_buckets = empty_buckets.at[expert_of, position].set(out_grad)
    grad_rows = lax.map(expert_backward, (buckets, grad_buckets, gate_weight, up_weight, down_weight))
    grad_normed = grad_rows[expert_of, position].astype(jnp.float32)
    scaled = grad_normed * norm_gain
    resid_grad = (out_grad.astype(jnp.float32) + inv_rms * (scaled - unit_rows * lax.optimization_barrier(jnp.mean(scaled * unit_rows, axis=-1, keepdims=True)))).astype(jnp.bfloat16)
    weight_grad = lax.dot_general(attended, resid_grad, (((0,), (0,)), ((), ())), preferred_element_type=jnp.float32)
    grad_attended = lax.dot_general(resid_grad, out_weight, (((1,), (1,)), ((), ())), preferred_element_type=jnp.float32).astype(jnp.bfloat16)
    query_grad, key_grad, value_grad = lax.map(seq_backward, (queries.reshape(tiled), attn_keys.reshape(tiled), attn_values.reshape(tiled), grad_attended.reshape(tiled)))
    return (layer_out, resid_grad, query_grad.reshape(TOKENS, A), key_grad.reshape(TOKENS, A), value_grad.reshape(TOKENS, A), weight_grad)
```

```python
import functools
import math

import jax
import jax.numpy as jnp
from jax import lax
from jax.experimental import pallas as pl
from jax.experimental.pallas import tpu as pltpu
from jax.sharding import PartitionSpec as P

D = 2048
HEADS = 8
HEAD = 128
A = 1024
FF = 4096


epsilon = 1e-06


def contract_last(left_side, right_side):
    return lax.dot_general(
        left_side, right_side, (((1,), (1,)), ((), ())), preferred_element_type=jnp.float32
    )


def contract_first(left_side, right_side):
    return lax.dot_general(
        left_side, right_side, (((0,), (0,)), ((), ())), preferred_element_type=jnp.float32
    )


MESH = pl.DeviceIdType.MESH
WHOLE = pl.BlockSpec(memory_space=pltpu.VMEM)


def flip(index, mask, size):
    total, bit = 0, 1
    while bit < size:
        here = lax.rem(lax.div(index, bit), 2)
        total = total + bit * ((1 - here) if (mask // bit) % 2 else here)
        bit *= 2
    return total


class Wire:
    def __init__(self, sizes, send_sems, recv_sems):
        self.sections, self.experts, self.ways = sizes
        self.outer = self.ways // 2
        self.section = lax.axis_index("section")
        self.expert = lax.axis_index("expert")
        self.dp = lax.axis_index("dp")
        self.low = lax.rem(self.dp, 2)
        self.high = lax.div(self.dp, 2)
        self.send_sems, self.recv_sems = send_sems, recv_sems
        self.started = []

    def send(self, source, target, peer):
        slot = len(self.started)
        copy = pltpu.make_async_remote_copy(
            src_ref=source,
            dst_ref=target,
            send_sem=self.send_sems.at[slot],
            recv_sem=self.recv_sems.at[slot],
            device_id=peer,
            device_id_type=MESH,
        )
        copy.start()
        self.started.append(copy)
        return copy

    def finish(self):
        for copy in self.started:
            copy.wait_send()

    def expert_at(self, mask):
        return flip(self.expert, mask, self.experts)

    def high_at(self, mask):
        return flip(self.high, mask, self.outer)

    def section_at(self, mask):
        return flip(self.section, mask, self.sections)

    def dp_at(self, mask):
        return self.high_at(mask) * 2 + self.low

    def to_expert(self, mask):
        return {"expert": self.expert_at(mask)}

    def to_high(self, mask):
        return {"dp": self.dp_at(mask)}

    def to_section(self, mask):
        return {"section": self.section_at(mask)}

    def to_low(self):
        return {"dp": self.high * 2 + (1 - self.low)}

    def expert_masks(self):
        half = self.experts // 2
        return list(range(half, self.experts)) + list(range(1, half))

    def greet(self, experts=True, sections=False):
        peers = [self.to_low()] + [self.to_high(m) for m in range(1, self.outer)]
        if experts:
            peers += [self.to_expert(m) for m in range(1, self.experts)]
        if sections:
            peers += [self.to_section(m) for m in range(1, self.sections)]
        barrier = pltpu.get_barrier_semaphore()
        for peer in peers:
            pl.semaphore_signal(barrier, inc=1, device_id=peer, device_id_type=MESH)
        pl.semaphore_wait(barrier, len(peers))


def added(first, *others):
    total = first.astype(jnp.float32)
    for other in others:
        total = total + other.astype(jnp.float32)
    return total.astype(jnp.bfloat16)


def gather_start(wire, block, out):
    wide = [wire.send(block, out.at[wire.dp], wire.to_high(m)) for m in range(1, wire.outer)]
    near = wire.send(block, out.at[wire.dp], wire.to_low())
    return wide, near


def gather_end(wire, flow, out):
    wide, near = flow
    passed = [near]
    for m, copy in enumerate(wide, 1):
        copy.wait_recv()
        block = out.at[wire.dp_at(m)]
        passed.append(wire.send(block, block, wire.to_low()))
    return passed


def cross(wire, source, out):
    return {
        m: wire.send(source.at[wire.expert_at(m)], out.at[wire.dp, wire.expert], wire.to_expert(m))
        for m in wire.expert_masks()
    }


def spread(wire, source, out, crossing):
    passed = []
    held = None

    def hand_over(mask, wide):
        for m, copy in enumerate(wide, 1):
            copy.wait_recv()
            block = out.at[wire.dp_at(m), wire.expert_at(mask)]
            passed.append(wire.send(block, block, wire.to_low()))

    for mask in [0] + wire.expert_masks():
        target = out.at[wire.dp, wire.expert_at(mask)]
        if mask:
            crossing[mask].wait_recv()
            block = target
        else:
            block = source.at[wire.expert]
        wide = [wire.send(block, target, wire.to_high(m)) for m in range(1, wire.outer)]
        passed.append(wire.send(block, target, wire.to_low()))
        if held is not None:
            hand_over(*held)
        held = (mask, wide)
    hand_over(*held)
    return passed


def settle(wire, passed):
    for copy in passed:
        copy.wait_recv()
    wire.finish()


def dispatch_kernel(sizes, rows, out, send_sems, recv_sems, own_sem):
    wire = Wire(sizes, send_sems, recv_sems)
    own = pltpu.make_async_copy(
        rows.at[wire.expert], out.at[wire.dp, wire.expert], own_sem
    )
    own.start()
    wire.greet()
    crossing = cross(wire, rows, out)
    passed = spread(wire, rows, out, crossing)
    settle(wire, passed)
    own.wait()


def opening_kernel(
    sizes, keys, values, weight, rows, keys_out, values_out, weight_out, out,
    send_sems, recv_sems, own_sems,
):
    wire = Wire(sizes, send_sems, recv_sems)
    local = [
        pltpu.make_async_copy(source, target, own_sems.at[i])
        for i, (source, target) in enumerate(
            (
                (keys, keys_out.at[wire.dp]),
                (values, values_out.at[wire.dp]),
                (weight, weight_out.at[wire.expert]),
                (rows.at[wire.expert], out.at[wire.dp, wire.expert]),
            )
        )
    ]
    for copy in local:
        copy.start()
    wire.greet(sections=True)
    key_flow = gather_start(wire, keys, keys_out)
    value_flow = gather_start(wire, values, values_out)
    part = wire.section * 2 + wire.low
    crossing = cross(wire, rows, out)
    quarters = {
        m: wire.send(weight.at[part], weight_out.at[wire.expert, part], wire.to_expert(m))
        for m in wire.expert_masks()
    }
    passed = gather_end(wire, key_flow, keys_out) + gather_end(wire, value_flow, values_out)
    passed += spread(wire, rows, out, crossing)
    sideways = {}
    for mask in wire.expert_masks():
        quarters[mask].wait_recv()
        block = weight_out.at[wire.expert_at(mask), part]
        sideways[mask] = [
            wire.send(block, block, wire.to_section(m)) for m in range(1, wire.sections)
        ]
        passed.append(wire.send(block, block, wire.to_low()))
    for mask in wire.expert_masks():
        for m, copy in enumerate(sideways[mask], 1):
            copy.wait_recv()
            block = weight_out.at[wire.expert_at(mask), wire.section_at(m) * 2 + wire.low]
            passed.append(wire.send(block, block, wire.to_low()))
    settle(wire, passed)
    for copy in local:
        copy.wait()


def fold_start(wire, parts, near_in, chunks):
    return {
        c: [
            wire.send(
                parts.at[h * 2 + (1 - wire.low), index],
                near_in.at[h, index],
                wire.to_low(),
            )
            for h in range(wire.outer)
        ]
        for c, index in chunks
    }


def fold_near(wire, flows, parts, near_in, far_in, c, index):
    for copy in flows[c]:
        copy.wait_recv()
    for h in range(wire.outer):
        near_in[h, index] = added(parts[h * 2 + wire.low, index], near_in[h, index])
    return [
        wire.send(near_in.at[wire.high_at(m), index], far_in.at[m - 1, index], wire.to_high(m))
        for m in range(1, wire.outer)
    ]


def fold_far(wire, far, near_in, far_in, index):
    for copy in far:
        copy.wait_recv()
    return added(
        near_in[wire.high, index], *[far_in[m - 1, index] for m in range(1, wire.outer)]
    )


def return_kernel(sizes, parts, out, near_in, far_in, total, send_sems, recv_sems):
    wire = Wire(sizes, send_sems, recv_sems)
    wire.greet()
    masks = wire.expert_masks() + [0]
    chunks = [(m, wire.expert_at(m)) for m in masks]
    flows = fold_start(wire, parts, near_in, chunks)
    far = {c: fold_near(wire, flows, parts, near_in, far_in, c, index) for c, index in chunks}
    arriving = []
    for c, index in chunks:
        summed = fold_far(wire, far[c], near_in, far_in, index)
        if c == 0:
            out[index] = summed
        else:
            total[index] = summed
            arriving.append(
                wire.send(total.at[index], out.at[wire.expert], wire.to_expert(c))
            )
    settle(wire, arriving)


def closing_kernel(
    sizes, parts, products, out, weight_out,
    near_in, far_in, low_in, side_in, high_in, total, cross_in, send_sems, recv_sems,
):
    wire = Wire(sizes, send_sems, recv_sems)
    wire.greet(sections=True)
    outer, sections = wire.outer, wire.sections
    span = outer * sections
    masks = wire.expert_masks() + [0]
    shards = [(m, wire.expert_at(m)) for m in masks]
    lows = {
        c: wire.send(
            products.at[pl.ds((1 - wire.low) * span, span), index],
            low_in.at[index],
            wire.to_low(),
        )
        for c, index in shards
    }
    pairs = [(i, i) for i in range(parts.shape[1])]
    flows = fold_start(wire, parts, near_in, pairs)
    sides = {}
    for c, index in shards:
        lows[c].wait_recv()
        for p in range(span):
            low_in[index, p] = added(products[wire.low * span + p, index], low_in[index, p])
        sides[c] = [
            wire.send(
                low_in.at[index, pl.ds(wire.section_at(m) * outer, outer)],
                side_in.at[m - 1, index],
                wire.to_section(m),
            )
            for m in range(1, sections)
        ]
    far = {c: fold_near(wire, flows, parts, near_in, far_in, c, index) for c, index in pairs}
    highs = {}
    for c, index in shards:
        for copy in sides[c]:
            copy.wait_recv()
        for h in range(outer):
            place = wire.section * outer + h
            low_in[index, place] = added(
                low_in[index, place], *[side_in[m - 1, index, h] for m in range(1, sections)]
            )
        highs[c] = [
            wire.send(
                low_in.at[index, wire.section * outer + wire.high_at(m)],
                high_in.at[m - 1, index],
                wire.to_high(m),
            )
            for m in range(1, outer)
        ]
    crossing = {}
    mine = None
    for c, index in shards:
        for copy in highs[c]:
            copy.wait_recv()
        summed = added(
            low_in[index, wire.section * outer + wire.high],
            *[high_in[m - 1, index] for m in range(1, outer)],
        )
        total[index] = summed
        if c:
            crossing[c] = wire.send(total.at[index], cross_in.at[c - 1], wire.to_expert(c))
    for c, index in pairs:
        out[index] = fold_far(wire, far[c], near_in, far_in, index)
    for c in crossing:
        crossing[c].wait_recv()
    place = wire.low * span + wire.section * outer + wire.high
    weight_out[place] = added(
        total[wire.expert], *[cross_in[m - 1] for m in range(1, wire.experts)]
    )
    base = wire.low * span
    passed = []
    wide = [
        wire.send(weight_out.at[place], weight_out.at[place], wire.to_high(m))
        for m in range(1, outer)
    ]
    side = [
        wire.send(weight_out.at[place], weight_out.at[place], wire.to_section(m))
        for m in range(1, sections)
    ]
    passed.append(wire.send(weight_out.at[place], weight_out.at[place], wire.to_low()))
    relayed = []
    for m, copy in enumerate(wide, 1):
        copy.wait_recv()
        block = weight_out.at[base + wire.section * outer + wire.high_at(m)]
        relayed += [
            (m, s, wire.send(block, block, wire.to_section(s))) for s in range(1, sections)
        ]
        passed.append(wire.send(block, block, wire.to_low()))
    for s, copy in enumerate(side, 1):
        copy.wait_recv()
        block = weight_out.at[base + wire.section_at(s) * outer + wire.high]
        passed.append(wire.send(block, block, wire.to_low()))
    for m, s, copy in relayed:
        copy.wait_recv()
        block = weight_out.at[base + wire.section_at(s) * outer + wire.high_at(m)]
        passed.append(wire.send(block, block, wire.to_low()))
    settle(wire, passed)


def call(kernel, sizes, ident, copies, operands, outs, scratch=(), extra=()):
    low = lambda shape: jax.ShapeDtypeStruct(shape, jnp.bfloat16)
    return pl.pallas_call(
        functools.partial(kernel, sizes),
        out_shape=[low(s) for s in outs],
        in_specs=[WHOLE] * len(operands),
        out_specs=[WHOLE] * len(outs),
        scratch_shapes=[pltpu.VMEM(s, jnp.bfloat16) for s in scratch]
        + [pltpu.SemaphoreType.DMA((copies,)), pltpu.SemaphoreType.DMA((copies,))]
        + list(extra),
        compiler_params=pltpu.CompilerParams(
            collective_id=ident, has_side_effects=True, vmem_limit_bytes=60 * 1024 * 1024
        ),
    )(*operands)


def shards(
    residual,
    queries,
    attn_keys,
    attn_values,
    out_weight,
    norm_gain,
    gate_weight,
    up_weight,
    down_weight,
    expert_ids,
    out_grad,
):
    tokens_here = residual.shape[0]
    experts = lax.axis_size("expert")
    data_ways = lax.axis_size("dp")
    capacity = max(tokens_here // 8, 2 * tokens_here // experts)
    inv_root = 1.0 / math.sqrt(HEAD)
    sections = lax.axis_size("section")
    sizes = (sections, experts, data_ways)
    outer = data_ways // 2
    expert_of = expert_ids[:, 0]
    onehot = (expert_of[:, None] == jnp.arange(experts, dtype=jnp.int32)[None, :]).astype(
        jnp.bfloat16
    )
    row_iota = jnp.arange(tokens_here, dtype=jnp.int32)
    earlier_mask = (row_iota[:, None] > row_iota[None, :]).astype(jnp.bfloat16)
    earlier = jnp.dot(earlier_mask, onehot, preferred_element_type=jnp.float32)
    rank_index = jnp.sum(earlier * onehot.astype(jnp.float32), axis=1).astype(jnp.int32)
    slot_index = expert_of * capacity + rank_index
    slot_iota = jnp.arange(experts * capacity, dtype=jnp.int32)
    placing = (slot_iota[:, None] == slot_index[None, :]).astype(jnp.bfloat16)
    buckets = (experts, capacity, D)
    spread_shape = (data_ways,) + buckets
    grad_buffer = jnp.dot(placing, out_grad).reshape(buckets)
    weight_rows = out_weight.shape[0]
    quarter = 2 * sections
    keys_all, values_all, full_out, grad_gathered = call(
        opening_kernel,
        sizes,
        0,
        4 * outer + experts * (1 + 2 * outer) + experts * (2 + 2 * sections),
        (
            attn_keys,
            attn_values,
            out_weight.reshape(quarter, weight_rows // quarter, D),
            grad_buffer,
        ),
        (
            (data_ways,) + attn_keys.shape,
            (data_ways,) + attn_values.shape,
            (experts, quarter, weight_rows // quarter, D),
            spread_shape,
        ),
        extra=(pltpu.SemaphoreType.DMA((4,)),),
    )
    full_out = full_out.reshape(A, D)
    query_heads = queries.reshape(tokens_here, HEADS, HEAD)
    key_heads = keys_all.reshape(-1, HEADS, HEAD)
    value_heads = values_all.reshape(-1, HEADS, HEAD)
    scores = (
        jnp.einsum("thd,shd->hts", query_heads, key_heads, preferred_element_type=jnp.float32)
        * inv_root
    )
    row_peak = jnp.max(scores, axis=-1, keepdims=True)
    exp_scores = jnp.exp(scores - row_peak)
    attn_probs = exp_scores / jnp.sum(exp_scores, axis=-1, keepdims=True)
    probs_low = attn_probs.astype(jnp.bfloat16)
    attended = (
        jnp.einsum("hts,shd->thd", probs_low, value_heads, preferred_element_type=jnp.float32)
        .reshape(tokens_here, A)
        .astype(jnp.bfloat16)
    )
    hidden = residual.astype(jnp.float32) + jnp.dot(
        attended, full_out, preferred_element_type=jnp.float32
    )
    inv_rms = lax.rsqrt(jnp.mean(hidden * hidden, axis=-1, keepdims=True) + epsilon)
    unit_rows = hidden * inv_rms
    normed = (unit_rows * norm_gain).astype(jnp.bfloat16)
    send_buffer = jnp.dot(placing, normed).reshape(buckets)
    gate_local = gate_weight[0]
    up_local = up_weight[0]
    down_local = down_weight[0]
    block_width = FF // data_ways
    (gathered,) = call(
        dispatch_kernel,
        sizes,
        1,
        experts * (1 + 2 * outer),
        (send_buffer,),
        (spread_shape,),
        extra=(pltpu.SemaphoreType.DMA,),
    )
    flattened = gathered.reshape(-1, D)
    gate_pre = jnp.dot(flattened, gate_local, preferred_element_type=jnp.float32)
    up_pre = jnp.dot(flattened, up_local, preferred_element_type=jnp.float32)
    activated = (jax.nn.silu(gate_pre) * up_pre).astype(jnp.bfloat16)
    partial_out = jnp.dot(activated, down_local, preferred_element_type=jnp.float32)
    back_copies = experts * (1 + outer + outer)
    back_scratch = ((outer,) + buckets, (max(outer - 1, 1),) + buckets, buckets)
    (returned,) = call(
        return_kernel,
        sizes,
        2,
        back_copies,
        (partial_out.astype(jnp.bfloat16).reshape(spread_shape),),
        (buckets,),
        back_scratch,
    )
    expert_back = contract_first(placing, returned.reshape(experts * capacity, D))
    layer_out = (hidden + expert_back.astype(jnp.float32)).astype(jnp.bfloat16)
    grad_flat = grad_gathered.reshape(-1, D)
    sigmoid_gate = jax.nn.sigmoid(gate_pre)
    grad_act = contract_last(grad_flat, down_local)
    grad_gate = (grad_act * up_pre * sigmoid_gate * (1.0 + gate_pre * (1.0 - sigmoid_gate))).astype(
        jnp.bfloat16
    )
    grad_up = (grad_act * jax.nn.silu(gate_pre)).astype(jnp.bfloat16)
    partial_grad = contract_last(grad_gate, gate_local) + contract_last(grad_up, up_local)
    (grad_returned,) = call(
        return_kernel,
        sizes,
        3,
        back_copies,
        (partial_grad.astype(jnp.bfloat16).reshape(spread_shape),),
        (buckets,),
        back_scratch,
    )
    grad_normed = contract_first(placing, grad_returned.reshape(experts * capacity, D))
    scaled = grad_normed * norm_gain
    resid_grad = (
        out_grad.astype(jnp.float32)
        + inv_rms * (scaled - unit_rows * jnp.mean(scaled * unit_rows, axis=-1, keepdims=True))
    ).astype(jnp.bfloat16)
    ways = data_ways * sections
    width = D // ways
    products = jnp.einsum(
        "ta,tpc->pac",
        attended,
        resid_grad.reshape(tokens_here, ways, width),
        preferred_element_type=jnp.float32,
    ).astype(jnp.bfloat16)
    grad_attended = contract_last(resid_grad, full_out).astype(jnp.bfloat16)
    grad_heads = grad_attended.reshape(tokens_here, HEADS, HEAD)
    grad_probs = jnp.einsum(
        "thd,shd->hts", grad_heads, value_heads, preferred_element_type=jnp.float32
    )
    row_delta = jnp.sum(attn_probs * grad_probs, axis=-1, keepdims=True)
    grad_scores = (attn_probs * (grad_probs - row_delta)).astype(jnp.bfloat16)
    query_grad = (
        (
            jnp.einsum("hts,shd->thd", grad_scores, key_heads, preferred_element_type=jnp.float32)
            * inv_root
        )
        .reshape(tokens_here, A)
        .astype(jnp.bfloat16)
    )
    key_part = (
        jnp.einsum("hts,thd->shd", grad_scores, query_heads, preferred_element_type=jnp.float32)
        * inv_root
    )
    value_part = jnp.einsum(
        "hts,thd->shd", probs_low, grad_heads, preferred_element_type=jnp.float32
    )
    pair_parts = jnp.stack(
        [
            key_part.reshape(data_ways, tokens_here, A),
            value_part.reshape(data_ways, tokens_here, A),
        ],
        axis=1,
    ).astype(jnp.bfloat16)
    pair = (2, tokens_here, A)
    block = (weight_rows, width)
    key_value, weight_parts = call(
        closing_kernel,
        sizes,
        4,
        4 * outer + experts * (1 + sections + outer + 1) + 3 * ways,
        (pair_parts, products.reshape(ways, experts, weight_rows, width)),
        (pair, (ways,) + block),
        (
            (outer,) + pair,
            (max(outer - 1, 1),) + pair,
            (experts, outer * sections) + block,
            (max(sections - 1, 1), experts, outer) + block,
            (max(outer - 1, 1), experts) + block,
            (experts,) + block,
            (experts - 1,) + block,
        ),
    )
    key_grad, value_grad = key_value[0], key_value[1]
    weight_grad = weight_parts.transpose(1, 0, 2).reshape(weight_rows, D).astype(jnp.float32)
    return (layer_out, resid_grad, query_grad, key_grad, value_grad, weight_grad)


def solution(mesh):
    return jax.shard_map(
        shards,
        mesh=mesh,
        in_specs=(
            P(("section", "expert", "dp"), None),
            P(("section", "expert", "dp"), None),
            P(("section", "expert", "dp"), None),
            P(("section", "expert", "dp"), None),
            P("expert", None),
            P(),
            P("expert", None, "dp"),
            P("expert", None, "dp"),
            P("expert", "dp", None),
            P(("section", "expert", "dp"), None),
            P(("section", "expert", "dp"), None),
        ),
        out_specs=(
            P(("section", "expert", "dp"), None),
            P(("section", "expert", "dp"), None),
            P(("section", "expert", "dp"), None),
            P(("section", "expert", "dp"), None),
            P(("section", "expert", "dp"), None),
            P("expert", None),
        ),
        check_vma=False,
    )
```

```python
import functools
import math

import jax
import jax.numpy as jnp
from jax import lax
from jax.experimental import pallas as pl
from jax.experimental.pallas import tpu as pltpu
from jax.sharding import PartitionSpec as P

D = 2048
HEADS = 8
HEAD = 128
A = 1024
FF = 4096


epsilon = 1e-06


def contract_last(left_side, right_side):
    return lax.dot_general(
        left_side, right_side, (((1,), (1,)), ((), ())), preferred_element_type=jnp.float32
    )


def contract_first(left_side, right_side):
    return lax.dot_general(
        left_side, right_side, (((0,), (0,)), ((), ())), preferred_element_type=jnp.float32
    )


MESH = pl.DeviceIdType.MESH
WHOLE = pl.BlockSpec(memory_space=pltpu.VMEM)


def flip(index, mask, size):
    total, bit = 0, 1
    while bit < size:
        total = total + bit * lax.rem(lax.div(index, bit) + (mask // bit), 2)
        bit *= 2
    return total


class Wire:
    def __init__(self, sizes, send_sems, recv_sems):
        self.sections, self.experts, self.ways = sizes
        self.outer = self.ways // 2
        self.section = lax.axis_index("section")
        self.expert = lax.axis_index("expert")
        self.dp = lax.axis_index("dp")
        self.low = lax.rem(self.dp, 2)
        self.high = lax.div(self.dp, 2)
        self.send_sems, self.recv_sems = send_sems, recv_sems
        self.started = []

    def send(self, source, target, peer):
        slot = len(self.started)
        copy = pltpu.make_async_remote_copy(
            src_ref=source,
            dst_ref=target,
            send_sem=self.send_sems.at[slot],
            recv_sem=self.recv_sems.at[slot],
            device_id=peer,
            device_id_type=MESH,
        )
        copy.start()
        self.started.append(copy)
        return copy

    def finish(self):
        for copy in self.started:
            copy.wait_send()

    def expert_at(self, mask):
        return flip(self.expert, mask, self.experts)

    def high_at(self, mask):
        return flip(self.high, mask, self.outer)

    def section_at(self, mask):
        return flip(self.section, mask, self.sections)

    def dp_at(self, mask):
        return self.high_at(mask) * 2 + self.low

    def to_expert(self, mask):
        return {"expert": self.expert_at(mask)}

    def to_high(self, mask):
        return {"dp": self.dp_at(mask)}

    def to_section(self, mask):
        return {"section": self.section_at(mask)}

    def to_low(self):
        return {"dp": self.high * 2 + (1 - self.low)}

    def expert_masks(self):
        half = self.experts // 2
        return list(range(half, self.experts)) + list(range(1, half))

    def greet(self, experts=True, sections=False):
        peers = [self.to_low()] + [self.to_high(m) for m in range(1, self.outer)]
        if experts:
            peers += [self.to_expert(m) for m in range(1, self.experts)]
        if sections:
            peers += [self.to_section(m) for m in range(1, self.sections)]
        barrier = pltpu.get_barrier_semaphore()
        for peer in peers:
            pl.semaphore_signal(barrier, inc=1, device_id=peer, device_id_type=MESH)
        pl.semaphore_wait(barrier, len(peers))


def added(first, *others):
    total = first.astype(jnp.float32)
    for other in others:
        total = total + other.astype(jnp.float32)
    return total.astype(jnp.bfloat16)


def gather_start(wire, block, out):
    wide = [wire.send(block, out.at[wire.dp], wire.to_high(m)) for m in range(1, wire.outer)]
    near = wire.send(block, out.at[wire.dp], wire.to_low())
    return wide, near


def gather_end(wire, flow, out):
    wide, near = flow
    passed = [near]
    for m, copy in enumerate(wide, 1):
        copy.wait_recv()
        block = out.at[wire.dp_at(m)]
        passed.append(wire.send(block, block, wire.to_low()))
    return passed


def cross(wire, source, out):
    return {
        m: wire.send(source.at[wire.expert_at(m)], out.at[wire.dp, wire.expert], wire.to_expert(m))
        for m in wire.expert_masks()
    }


def spread(wire, source, out, crossing):
    passed = []
    held = None

    def hand_over(mask, wide):
        for m, copy in enumerate(wide, 1):
            copy.wait_recv()
            block = out.at[wire.dp_at(m), wire.expert_at(mask)]
            passed.append(wire.send(block, block, wire.to_low()))

    for mask in [0] + wire.expert_masks():
        target = out.at[wire.dp, wire.expert_at(mask)]
        if mask:
            crossing[mask].wait_recv()
            block = target
        else:
            block = source.at[wire.expert]
        wide = [wire.send(block, target, wire.to_high(m)) for m in range(1, wire.outer)]
        passed.append(wire.send(block, target, wire.to_low()))
        if held is not None:
            hand_over(*held)
        held = (mask, wide)
    hand_over(*held)
    return passed


def settle(wire, passed):
    for copy in passed:
        copy.wait_recv()
    wire.finish()


def opening_kernel(
    sizes, keys, values, weight, rows, keys_out, values_out, weight_out, out,
    send_sems, recv_sems, own_sems,
):
    wire = Wire(sizes, send_sems, recv_sems)
    local = [
        pltpu.make_async_copy(source, target, own_sems.at[i])
        for i, (source, target) in enumerate(
            (
                (keys, keys_out.at[wire.dp]),
                (values, values_out.at[wire.dp]),
                (weight, weight_out.at[wire.expert]),
                (rows.at[wire.expert], out.at[wire.dp, wire.expert]),
            )
        )
    ]
    for copy in local:
        copy.start()
    wire.greet(sections=True)
    key_flow = gather_start(wire, keys, keys_out)
    value_flow = gather_start(wire, values, values_out)
    part = wire.section * 2 + wire.low
    crossing = cross(wire, rows, out)
    quarters = {
        m: wire.send(weight.at[part], weight_out.at[wire.expert, part], wire.to_expert(m))
        for m in wire.expert_masks()
    }
    passed = gather_end(wire, key_flow, keys_out) + gather_end(wire, value_flow, values_out)
    passed += spread(wire, rows, out, crossing)
    sideways = {}
    for mask in wire.expert_masks():
        quarters[mask].wait_recv()
        block = weight_out.at[wire.expert_at(mask), part]
        sideways[mask] = [
            wire.send(block, block, wire.to_section(m)) for m in range(1, wire.sections)
        ]
        passed.append(wire.send(block, block, wire.to_low()))
    for mask in wire.expert_masks():
        for m, copy in enumerate(sideways[mask], 1):
            copy.wait_recv()
            block = weight_out.at[wire.expert_at(mask), wire.section_at(m) * 2 + wire.low]
            passed.append(wire.send(block, block, wire.to_low()))
    settle(wire, passed)
    for copy in local:
        copy.wait()


def fold_start(wire, parts, near_in, chunks):
    return {
        c: [
            wire.send(
                parts.at[h * 2 + (1 - wire.low), index],
                near_in.at[h, index],
                wire.to_low(),
            )
            for h in range(wire.outer)
        ]
        for c, index in chunks
    }


def fold_near(wire, flows, parts, near_in, far_in, c, index):
    for copy in flows[c]:
        copy.wait_recv()
    for h in range(wire.outer):
        near_in[h, index] = added(parts[h * 2 + wire.low, index], near_in[h, index])
    return [
        wire.send(near_in.at[wire.high_at(m), index], far_in.at[m - 1, index], wire.to_high(m))
        for m in range(1, wire.outer)
    ]


def fold_far(wire, far, near_in, far_in, index):
    for copy in far:
        copy.wait_recv()
    return added(
        near_in[wire.high, index], *[far_in[m - 1, index] for m in range(1, wire.outer)]
    )


def closing_kernel(
    sizes, parts, products, out, weight_out,
    near_in, far_in, low_in, side_in, high_in, total, cross_in, send_sems, recv_sems,
):
    wire = Wire(sizes, send_sems, recv_sems)
    wire.greet(sections=True)
    outer, sections = wire.outer, wire.sections
    span = outer * sections
    masks = wire.expert_masks() + [0]
    shards = [(m, wire.expert_at(m)) for m in masks]
    lows = {
        c: wire.send(
            products.at[pl.ds((1 - wire.low) * span, span), index],
            low_in.at[index],
            wire.to_low(),
        )
        for c, index in shards
    }
    pairs = [(i, i) for i in range(parts.shape[1])]
    flows = fold_start(wire, parts, near_in, pairs)
    sides = {}
    for c, index in shards:
        lows[c].wait_recv()
        for p in range(span):
            low_in[index, p] = added(products[wire.low * span + p, index], low_in[index, p])
        sides[c] = [
            wire.send(
                low_in.at[index, pl.ds(wire.section_at(m) * outer, outer)],
                side_in.at[m - 1, index],
                wire.to_section(m),
            )
            for m in range(1, sections)
        ]
    far = {c: fold_near(wire, flows, parts, near_in, far_in, c, index) for c, index in pairs}
    highs = {}
    for c, index in shards:
        for copy in sides[c]:
            copy.wait_recv()
        for h in range(outer):
            place = wire.section * outer + h
            low_in[index, place] = added(
                low_in[index, place], *[side_in[m - 1, index, h] for m in range(1, sections)]
            )
        highs[c] = [
            wire.send(
                low_in.at[index, wire.section * outer + wire.high_at(m)],
                high_in.at[m - 1, index],
                wire.to_high(m),
            )
            for m in range(1, outer)
        ]
    crossing = {}
    mine = None
    for c, index in shards:
        for copy in highs[c]:
            copy.wait_recv()
        summed = added(
            low_in[index, wire.section * outer + wire.high],
            *[high_in[m - 1, index] for m in range(1, outer)],
        )
        total[index] = summed
        if c:
            crossing[c] = wire.send(total.at[index], cross_in.at[c - 1], wire.to_expert(c))
    for c, index in pairs:
        out[index] = fold_far(wire, far[c], near_in, far_in, index)
    for c in crossing:
        crossing[c].wait_recv()
    place = wire.low * span + wire.section * outer + wire.high
    weight_out[place] = added(
        total[wire.expert], *[cross_in[m - 1] for m in range(1, wire.experts)]
    )
    base = wire.low * span
    passed = []
    wide = [
        wire.send(weight_out.at[place], weight_out.at[place], wire.to_high(m))
        for m in range(1, outer)
    ]
    side = [
        wire.send(weight_out.at[place], weight_out.at[place], wire.to_section(m))
        for m in range(1, sections)
    ]
    passed.append(wire.send(weight_out.at[place], weight_out.at[place], wire.to_low()))
    relayed = []
    for m, copy in enumerate(wide, 1):
        copy.wait_recv()
        block = weight_out.at[base + wire.section * outer + wire.high_at(m)]
        relayed += [
            (m, s, wire.send(block, block, wire.to_section(s))) for s in range(1, sections)
        ]
        passed.append(wire.send(block, block, wire.to_low()))
    for s, copy in enumerate(side, 1):
        copy.wait_recv()
        block = weight_out.at[base + wire.section_at(s) * outer + wire.high]
        passed.append(wire.send(block, block, wire.to_low()))
    for m, s, copy in relayed:
        copy.wait_recv()
        block = weight_out.at[base + wire.section_at(s) * outer + wire.high_at(m)]
        passed.append(wire.send(block, block, wire.to_low()))
    settle(wire, passed)


def call(kernel, sizes, ident, copies, operands, outs, scratch=(), extra=()):
    low = lambda shape: jax.ShapeDtypeStruct(shape, jnp.bfloat16)
    return pl.pallas_call(
        functools.partial(kernel, sizes),
        out_shape=[low(s) for s in outs],
        in_specs=[WHOLE] * len(operands),
        out_specs=[WHOLE] * len(outs),
        scratch_shapes=[pltpu.VMEM(s, jnp.bfloat16) for s in scratch]
        + [pltpu.SemaphoreType.DMA((copies,)), pltpu.SemaphoreType.DMA((copies,))]
        + list(extra),
        compiler_params=pltpu.CompilerParams(
            collective_id=ident, has_side_effects=True, vmem_limit_bytes=60 * 1024 * 1024
        ),
    )(*operands)


def expert_kernel(
    sizes, rows, grads, gate_hbm, up_hbm, down_hbm, grad_back, back,
    gathered, gate, up, down, act, gate_grad, up_grad, parts, near_in, far_in, total,
    zs, zr, hs, hr, ls, lr, fls, flr, fhs, fhr, fzs, fzr, weight_sems, own_sem,
):
    wire = Wire(sizes, None, None)
    experts, outer, ways = wire.experts, wire.outer, wire.ways
    capacity, width = rows.shape[1], rows.shape[2]
    hidden_units = gate.shape[1]
    backs = (grad_back, back)
    loads = [
        pltpu.make_async_copy(source.at[0], target, weight_sems.at[i])
        for i, (source, target) in enumerate(((gate_hbm, gate), (up_hbm, up), (down_hbm, down)))
    ]
    own = pltpu.make_async_copy(
        rows.at[wire.expert], gathered.at[wire.dp, wire.expert], own_sem
    )
    own.start()
    for load in loads:
        load.start()
    wire.greet()

    def link(source, target, send_sem, recv_sem, peer):
        return pltpu.make_async_remote_copy(
            src_ref=source, dst_ref=target, send_sem=send_sem, recv_sem=recv_sem,
            device_id=peer, device_id_type=MESH,
        )

    def over_expert(mask):
        return link(
            rows.at[wire.expert_at(mask)], gathered.at[wire.dp, wire.expert],
            zs.at[mask], zr.at[mask], wire.to_expert(mask),
        )

    def over_high(m, mask):
        block = gathered.at[wire.dp, wire.expert_at(mask)]
        return link(block, block, hs.at[m - 1, mask], hr.at[m - 1, mask], wire.to_high(m))

    def over_low(m, mask):
        block = gathered.at[wire.dp_at(m) if m else wire.dp, wire.expert_at(mask)]
        return link(block, block, ls.at[m, mask], lr.at[m, mask], wire.to_low())

    def back_low(r, h, mask):
        index = wire.expert_at(mask)
        return link(
            parts.at[r, h * 2 + (1 - wire.low), index], near_in.at[r, h, index],
            fls.at[r, h, mask], flr.at[r, h, mask], wire.to_low(),
        )

    def back_high(r, m, mask):
        index = wire.expert_at(mask)
        return link(
            near_in.at[r, wire.high_at(m), index], far_in.at[r, m - 1, index],
            fhs.at[r, m - 1, mask], fhr.at[r, m - 1, mask], wire.to_high(m),
        )

    def back_expert(r, mask):
        index = wire.expert_at(mask)
        return link(
            total.at[r, index], backs[r].at[wire.expert],
            fzs.at[r, mask], fzr.at[r, mask], wire.to_expert(mask),
        )

    def fold_low(r, mask):
        index = wire.expert_at(mask)
        for h in range(outer):
            back_low(r, h, mask).wait_recv()
            near_in[r, h, index] = added(parts[r, h * 2 + wire.low, index], near_in[r, h, index])
        for m in range(1, outer):
            back_high(r, m, mask).start()

    def fold_high(r, mask, position):
        index = wire.expert_at(mask)
        for m in range(1, outer):
            back_high(r, m, mask).wait_recv()
        summed = added(
            near_in[r, wire.high, index], *[far_in[r, m - 1, index] for m in range(1, outer)]
        )

        @pl.when(position == 0)
        def _():
            backs[r][index] = summed

        @pl.when(position > 0)
        def _():
            total[r, index] = summed
            back_expert(r, mask).start()

    tile = 256

    def units(mask):
        index = wire.expert_at(mask)

        @pl.loop(0, hidden_units // tile)
        def _(j):
            columns = pl.ds(pl.multiple_of(j * tile, tile), tile)
            block = gathered[:, index].reshape(ways * capacity, width)
            grad_block = grads[:, index].reshape(ways * capacity, width)
            gate_pre = jnp.dot(block, gate[:, columns], preferred_element_type=jnp.float32)
            up_pre = jnp.dot(block, up[:, columns], preferred_element_type=jnp.float32)
            grad_act = contract_last(grad_block, down[columns, :])
            sigmoid_gate = jax.nn.sigmoid(gate_pre)
            silu = gate_pre * sigmoid_gate
            act[:, columns] = (silu * up_pre).astype(jnp.bfloat16)
            gate_grad[:, columns] = (
                grad_act * up_pre * sigmoid_gate * (1.0 + gate_pre * (1.0 - sigmoid_gate))
            ).astype(jnp.bfloat16)
            up_grad[:, columns] = (grad_act * silu).astype(jnp.bfloat16)

    def grad_products(mask):
        index = wire.expert_at(mask)

        @pl.loop(0, width // tile)
        def _(j):
            columns = pl.ds(pl.multiple_of(j * tile, tile), tile)
            piece = contract_last(gate_grad[...], gate[columns, :]) + contract_last(
                up_grad[...], up[columns, :]
            )
            parts[0, :, index, :, columns] = piece.astype(jnp.bfloat16).reshape(
                ways, capacity, tile
            )

    def out_products(mask):
        index = wire.expert_at(mask)

        @pl.loop(0, width // tile)
        def _(j):
            columns = pl.ds(pl.multiple_of(j * tile, tile), tile)
            piece = jnp.dot(act[...], down[:, columns], preferred_element_type=jnp.float32)
            parts[1, :, index, :, columns] = piece.astype(jnp.bfloat16).reshape(
                ways, capacity, tile
            )

    for step in range(1, experts):
        over_expert(experts - step).start()
    own.wait()

    def mask_of(position):
        return lax.rem(experts - position, experts)

    @pl.loop(0, experts + 2)
    def _(step):
        incoming, current, leaving = step < experts, step >= 1, step >= 2
        now, before, last = mask_of(step), mask_of(step - 1), mask_of(step - 2)

        @pl.when(incoming)
        def _():
            @pl.when(step > 0)
            def _():
                over_expert(now).wait_recv()

            for m in range(1, outer):
                over_high(m, now).start()
            over_low(0, now).start()

        @pl.when(leaving)
        def _():
            fold_low(1, last)

        @pl.when(step == 1)
        def _():
            for load in loads:
                load.wait()

        busy = current & (step <= experts)

        @pl.when(busy)
        def _():
            for m in range(outer):
                over_low(m, before).wait_recv()
            units(before)
            grad_products(before)
            for h in range(outer):
                back_low(0, h, before).start()

        @pl.when(incoming)
        def _():
            for m in range(1, outer):
                over_high(m, now).wait_recv()
                over_low(m, now).start()

        @pl.when(leaving)
        def _():
            fold_high(0, last, step - 2)

        @pl.when(busy)
        def _():
            out_products(before)
            fold_low(0, before)
            for h in range(outer):
                back_low(1, h, before).start()

        @pl.when(leaving)
        def _():
            fold_high(1, last, step - 2)

    for mask in range(experts):
        for r in range(2):
            if mask:
                back_expert(r, mask).wait()
            for h in range(outer):
                back_low(r, h, mask).wait_send()
            for m in range(1, outer):
                back_high(r, m, mask).wait_send()
        if mask:
            over_expert(mask).wait_send()
        for m in range(1, outer):
            over_high(m, mask).wait_send()
        for m in range(outer):
            over_low(m, mask).wait_send()


def run_experts(sizes, ident, rows, grads, gate_weight, up_weight, down_weight):
    sections, experts, ways = sizes
    outer = ways // 2
    span = max(outer - 1, 1)
    buckets = rows.shape
    count = ways * buckets[1]
    units = gate_weight.shape[2]
    anywhere = pl.BlockSpec(memory_space=pl.ANY)
    low = lambda *shape: pltpu.VMEM(shape, jnp.bfloat16)
    sems = []
    for shape in (
        (experts,),
        (span, experts),
        (outer, experts),
        (2, outer, experts),
        (2, span, experts),
        (2, experts),
    ):
        sems += [pltpu.SemaphoreType.DMA(shape)] * 2
    return pl.pallas_call(
        functools.partial(expert_kernel, sizes),
        out_shape=[jax.ShapeDtypeStruct(buckets, jnp.bfloat16)] * 2,
        in_specs=[WHOLE, WHOLE, anywhere, anywhere, anywhere],
        out_specs=[WHOLE, WHOLE],
        scratch_shapes=[
            low(ways, *buckets),
            low(*gate_weight.shape[1:]),
            low(*up_weight.shape[1:]),
            low(*down_weight.shape[1:]),
            low(count, units),
            low(count, units),
            low(count, units),
            low(2, ways, *buckets),
            low(2, outer, *buckets),
            low(2, span, *buckets),
            low(2, *buckets),
        ]
        + sems
        + [pltpu.SemaphoreType.DMA((3,)), pltpu.SemaphoreType.DMA],
        compiler_params=pltpu.CompilerParams(
            collective_id=ident, has_side_effects=True, vmem_limit_bytes=62 * 1024 * 1024
        ),
    )(rows, grads, gate_weight, up_weight, down_weight)


def shards(
    residual,
    queries,
    attn_keys,
    attn_values,
    out_weight,
    norm_gain,
    gate_weight,
    up_weight,
    down_weight,
    expert_ids,
    out_grad,
):
    tokens_here = residual.shape[0]
    experts = lax.axis_size("expert")
    data_ways = lax.axis_size("dp")
    capacity = max(tokens_here // 8, 2 * tokens_here // experts)
    inv_root = 1.0 / math.sqrt(HEAD)
    sections = lax.axis_size("section")
    sizes = (sections, experts, data_ways)
    outer = data_ways // 2
    expert_of = expert_ids[:, 0]
    onehot = (expert_of[:, None] == jnp.arange(experts, dtype=jnp.int32)[None, :]).astype(
        jnp.bfloat16
    )
    row_iota = jnp.arange(tokens_here, dtype=jnp.int32)
    earlier_mask = (row_iota[:, None] > row_iota[None, :]).astype(jnp.bfloat16)
    earlier = jnp.dot(earlier_mask, onehot, preferred_element_type=jnp.float32)
    rank_index = jnp.sum(earlier * onehot.astype(jnp.float32), axis=1).astype(jnp.int32)
    slot_index = expert_of * capacity + rank_index
    slot_iota = jnp.arange(experts * capacity, dtype=jnp.int32)
    placing = (slot_iota[:, None] == slot_index[None, :]).astype(jnp.bfloat16)
    buckets = (experts, capacity, D)
    spread_shape = (data_ways,) + buckets
    grad_buffer = jnp.dot(placing, out_grad).reshape(buckets)
    weight_rows = out_weight.shape[0]
    quarter = 2 * sections
    keys_all, values_all, full_out, grad_gathered = call(
        opening_kernel,
        sizes,
        0,
        4 * outer + experts * (1 + 2 * outer) + experts * (2 + 2 * sections),
        (
            attn_keys,
            attn_values,
            out_weight.reshape(quarter, weight_rows // quarter, D),
            grad_buffer,
        ),
        (
            (data_ways,) + attn_keys.shape,
            (data_ways,) + attn_values.shape,
            (experts, quarter, weight_rows // quarter, D),
            spread_shape,
        ),
        extra=(pltpu.SemaphoreType.DMA((4,)),),
    )
    full_out = full_out.reshape(A, D)
    query_heads = queries.reshape(tokens_here, HEADS, HEAD)
    key_heads = keys_all.reshape(-1, HEADS, HEAD)
    value_heads = values_all.reshape(-1, HEADS, HEAD)
    scores = (
        jnp.einsum("thd,shd->hts", query_heads, key_heads, preferred_element_type=jnp.float32)
        * inv_root
    )
    row_peak = jnp.max(scores, axis=-1, keepdims=True)
    exp_scores = jnp.exp(scores - row_peak)
    attn_probs = exp_scores / jnp.sum(exp_scores, axis=-1, keepdims=True)
    probs_low = attn_probs.astype(jnp.bfloat16)
    attended = (
        jnp.einsum("hts,shd->thd", probs_low, value_heads, preferred_element_type=jnp.float32)
        .reshape(tokens_here, A)
        .astype(jnp.bfloat16)
    )
    hidden = residual.astype(jnp.float32) + jnp.dot(
        attended, full_out, preferred_element_type=jnp.float32
    )
    inv_rms = lax.rsqrt(jnp.mean(hidden * hidden, axis=-1, keepdims=True) + epsilon)
    unit_rows = hidden * inv_rms
    normed = (unit_rows * norm_gain).astype(jnp.bfloat16)
    send_buffer = jnp.dot(placing, normed).reshape(buckets)
    grad_returned, returned = run_experts(
        sizes, 1, send_buffer, grad_gathered, gate_weight, up_weight, down_weight
    )
    expert_back = contract_first(placing, returned.reshape(experts * capacity, D))
    layer_out = (hidden + expert_back.astype(jnp.float32)).astype(jnp.bfloat16)
    grad_normed = contract_first(placing, grad_returned.reshape(experts * capacity, D))
    scaled = grad_normed * norm_gain
    resid_grad = (
        out_grad.astype(jnp.float32)
        + inv_rms * (scaled - unit_rows * jnp.mean(scaled * unit_rows, axis=-1, keepdims=True))
    ).astype(jnp.bfloat16)
    ways = data_ways * sections
    width = D // ways
    products = jnp.einsum(
        "ta,tpc->pac",
        attended,
        resid_grad.reshape(tokens_here, ways, width),
        preferred_element_type=jnp.float32,
    ).astype(jnp.bfloat16)
    grad_attended = contract_last(resid_grad, full_out).astype(jnp.bfloat16)
    grad_heads = grad_attended.reshape(tokens_here, HEADS, HEAD)
    grad_probs = jnp.einsum(
        "thd,shd->hts", grad_heads, value_heads, preferred_element_type=jnp.float32
    )
    row_delta = jnp.sum(attn_probs * grad_probs, axis=-1, keepdims=True)
    grad_scores = (attn_probs * (grad_probs - row_delta)).astype(jnp.bfloat16)
    query_grad = (
        (
            jnp.einsum("hts,shd->thd", grad_scores, key_heads, preferred_element_type=jnp.float32)
            * inv_root
        )
        .reshape(tokens_here, A)
        .astype(jnp.bfloat16)
    )
    key_part = (
        jnp.einsum("hts,thd->shd", grad_scores, query_heads, preferred_element_type=jnp.float32)
        * inv_root
    )
    value_part = jnp.einsum(
        "hts,thd->shd", probs_low, grad_heads, preferred_element_type=jnp.float32
    )
    pair_parts = jnp.stack(
        [
            key_part.reshape(data_ways, tokens_here, A),
            value_part.reshape(data_ways, tokens_here, A),
        ],
        axis=1,
    ).astype(jnp.bfloat16)
    pair = (2, tokens_here, A)
    block = (weight_rows, width)
    key_value, weight_parts = call(
        closing_kernel,
        sizes,
        2,
        4 * outer + experts * (1 + sections + outer + 1) + 3 * ways,
        (pair_parts, products.reshape(ways, experts, weight_rows, width)),
        (pair, (ways,) + block),
        (
            (outer,) + pair,
            (max(outer - 1, 1),) + pair,
            (experts, outer * sections) + block,
            (max(sections - 1, 1), experts, outer) + block,
            (max(outer - 1, 1), experts) + block,
            (experts,) + block,
            (experts - 1,) + block,
        ),
    )
    key_grad, value_grad = key_value[0], key_value[1]
    weight_grad = weight_parts.transpose(1, 0, 2).reshape(weight_rows, D).astype(jnp.float32)
    return (layer_out, resid_grad, query_grad, key_grad, value_grad, weight_grad)


def solution(mesh):
    return jax.shard_map(
        shards,
        mesh=mesh,
        in_specs=(
            P(("section", "expert", "dp"), None),
            P(("section", "expert", "dp"), None),
            P(("section", "expert", "dp"), None),
            P(("section", "expert", "dp"), None),
            P("expert", None),
            P(),
            P("expert", None, "dp"),
            P("expert", None, "dp"),
            P("expert", "dp", None),
            P(("section", "expert", "dp"), None),
            P(("section", "expert", "dp"), None),
        ),
        out_specs=(
            P(("section", "expert", "dp"), None),
            P(("section", "expert", "dp"), None),
            P(("section", "expert", "dp"), None),
            P(("section", "expert", "dp"), None),
            P(("section", "expert", "dp"), None),
            P("expert", None),
        ),
        check_vma=False,
    )
```

```python
import functools
import math

import jax
import jax.numpy as jnp
from jax import lax
from jax.experimental import pallas as pl
from jax.experimental.pallas import tpu as pltpu
from jax.sharding import PartitionSpec as P

D = 2048
HEADS = 8
HEAD = 128
A = 1024
FF = 4096


epsilon = 1e-06


def contract_last(left_side, right_side):
    return lax.dot_general(
        left_side, right_side, (((1,), (1,)), ((), ())), preferred_element_type=jnp.float32
    )


def contract_first(left_side, right_side):
    return lax.dot_general(
        left_side, right_side, (((0,), (0,)), ((), ())), preferred_element_type=jnp.float32
    )


MESH = pl.DeviceIdType.MESH
WHOLE = pl.BlockSpec(memory_space=pltpu.VMEM)


def flip(index, mask, size):
    total, bit = 0, 1
    while bit < size:
        total = total + bit * lax.rem(lax.div(index, bit) + (mask // bit), 2)
        bit *= 2
    return total


class Wire:
    def __init__(self, sizes, send_sems, recv_sems):
        self.sections, self.experts, self.ways = sizes
        self.outer = self.ways // 2
        self.section = lax.axis_index("section")
        self.expert = lax.axis_index("expert")
        self.dp = lax.axis_index("dp")
        self.low = lax.rem(self.dp, 2)
        self.high = lax.div(self.dp, 2)
        self.send_sems, self.recv_sems = send_sems, recv_sems
        self.started = []

    def send(self, source, target, peer):
        slot = len(self.started)
        copy = pltpu.make_async_remote_copy(
            src_ref=source,
            dst_ref=target,
            send_sem=self.send_sems.at[slot],
            recv_sem=self.recv_sems.at[slot],
            device_id=peer,
            device_id_type=MESH,
        )
        copy.start()
        self.started.append(copy)
        return copy

    def finish(self):
        for copy in self.started:
            copy.wait_send()

    def expert_at(self, mask):
        return flip(self.expert, mask, self.experts)

    def high_at(self, mask):
        return flip(self.high, mask, self.outer)

    def section_at(self, mask):
        return flip(self.section, mask, self.sections)

    def dp_at(self, mask):
        return self.high_at(mask) * 2 + self.low

    def to_expert(self, mask):
        return {"expert": self.expert_at(mask)}

    def to_high(self, mask):
        return {"dp": self.dp_at(mask)}

    def to_section(self, mask):
        return {"section": self.section_at(mask)}

    def to_low(self):
        return {"dp": self.high * 2 + (1 - self.low)}

    def expert_masks(self):
        half = self.experts // 2
        return list(range(half, self.experts)) + list(range(1, half))

    def greet(self, experts=True, sections=False):
        peers = [self.to_low()] + [self.to_high(m) for m in range(1, self.outer)]
        if experts:
            peers += [self.to_expert(m) for m in range(1, self.experts)]
        if sections:
            peers += [self.to_section(m) for m in range(1, self.sections)]
        barrier = pltpu.get_barrier_semaphore()
        for peer in peers:
            pl.semaphore_signal(barrier, inc=1, device_id=peer, device_id_type=MESH)
        pl.semaphore_wait(barrier, len(peers))


def added(first, *others):
    total = first.astype(jnp.float32)
    for other in others:
        total = total + other.astype(jnp.float32)
    return total.astype(jnp.bfloat16)


def gather_start(wire, block, out):
    wide = [wire.send(block, out.at[wire.dp], wire.to_high(m)) for m in range(1, wire.outer)]
    near = wire.send(block, out.at[wire.dp], wire.to_low())
    return wide, near


def gather_end(wire, flow, out):
    wide, near = flow
    passed = [near]
    for m, copy in enumerate(wide, 1):
        copy.wait_recv()
        block = out.at[wire.dp_at(m)]
        passed.append(wire.send(block, block, wire.to_low()))
    return passed


def cross(wire, source, out):
    return {
        m: wire.send(source.at[wire.expert_at(m)], out.at[wire.dp, wire.expert], wire.to_expert(m))
        for m in wire.expert_masks()
    }


def spread_own(wire, source, out):
    block, target = source.at[wire.expert], out.at[wire.dp, wire.expert]
    wide = [wire.send(block, target, wire.to_high(m)) for m in range(1, wire.outer)]
    return wide, wire.send(block, target, wire.to_low())


def spread(wire, out, crossing, first):
    passed = [first[1]]
    held = (0, first[0])

    def hand_over(mask, wide):
        for m, copy in enumerate(wide, 1):
            copy.wait_recv()
            block = out.at[wire.dp_at(m), wire.expert_at(mask)]
            passed.append(wire.send(block, block, wire.to_low()))

    for mask in wire.expert_masks():
        block = out.at[wire.dp, wire.expert_at(mask)]
        crossing[mask].wait_recv()
        wide = [wire.send(block, block, wire.to_high(m)) for m in range(1, wire.outer)]
        passed.append(wire.send(block, block, wire.to_low()))
        hand_over(*held)
        held = (mask, wide)
    hand_over(*held)
    return passed


def settle(wire, passed):
    for copy in passed:
        copy.wait_recv()
    wire.finish()


def opening_kernel(
    sizes, keys, values, weight, rows, keys_out, values_out, weight_out, out,
    send_sems, recv_sems, own_sems,
):
    wire = Wire(sizes, send_sems, recv_sems)
    local = [
        pltpu.make_async_copy(source, target, own_sems.at[i])
        for i, (source, target) in enumerate(
            (
                (keys, keys_out.at[wire.dp]),
                (values, values_out.at[wire.dp]),
                (weight, weight_out.at[wire.expert]),
                (rows.at[wire.expert], out.at[wire.dp, wire.expert]),
            )
        )
    ]
    for copy in local:
        copy.start()
    wire.greet(sections=True)
    key_flow = gather_start(wire, keys, keys_out)
    value_flow = gather_start(wire, values, values_out)
    outer, sections = wire.outer, wire.sections

    def piece(mask, section, high):
        return weight_out.at[wire.expert_at(mask), (section * 2 + wire.low) * outer + high]

    part = (wire.section * 2 + wire.low) * outer + wire.high
    pieces = {
        m: wire.send(weight.at[part], weight_out.at[wire.expert, part], wire.to_expert(m))
        for m in wire.expert_masks()
    }
    crossing = cross(wire, rows, out)
    passed = gather_end(wire, key_flow, keys_out) + gather_end(wire, value_flow, values_out)
    wides, sides = [], []
    for mask in wire.expert_masks():
        pieces[mask].wait_recv()
        block = piece(mask, wire.section, wire.high)
        for m in range(1, outer):
            wides.append((mask, m, wire.send(block, block, wire.to_high(m))))
        for s in range(1, sections):
            sides.append((mask, 0, s, wire.send(block, block, wire.to_section(s))))
        passed.append(wire.send(block, block, wire.to_low()))
    first = spread_own(wire, rows, out)
    for mask, m, copy in wides:
        copy.wait_recv()
        block = piece(mask, wire.section, wire.high_at(m))
        for s in range(1, sections):
            sides.append((mask, m, s, wire.send(block, block, wire.to_section(s))))
        passed.append(wire.send(block, block, wire.to_low()))
    passed += spread(wire, out, crossing, first)
    for mask, m, s, copy in sides:
        copy.wait_recv()
        block = piece(mask, wire.section_at(s), wire.high_at(m) if m else wire.high)
        passed.append(wire.send(block, block, wire.to_low()))
    settle(wire, passed)
    for copy in local:
        copy.wait()


def fold_start(wire, parts, near_in, chunks):
    return {
        c: [
            wire.send(
                parts.at[h * 2 + (1 - wire.low), index],
                near_in.at[h, index],
                wire.to_low(),
            )
            for h in range(wire.outer)
        ]
        for c, index in chunks
    }


def fold_near(wire, flows, parts, near_in, far_in, c, index):
    for copy in flows[c]:
        copy.wait_recv()
    for h in range(wire.outer):
        near_in[h, index] = added(parts[h * 2 + wire.low, index], near_in[h, index])
    return [
        wire.send(near_in.at[wire.high_at(m), index], far_in.at[m - 1, index], wire.to_high(m))
        for m in range(1, wire.outer)
    ]


def fold_far(wire, far, near_in, far_in, index):
    for copy in far:
        copy.wait_recv()
    return added(
        near_in[wire.high, index], *[far_in[m - 1, index] for m in range(1, wire.outer)]
    )


def closing_kernel(
    sizes, parts, features, columns, out, weight_out,
    near_in, far_in, columns_in, total, cross_in, send_sems, recv_sems, own_sem,
):
    wire = Wire(sizes, send_sems, recv_sems)
    outer, sections = wire.outer, wire.sections
    span = outer * sections

    def at(flip_low, s, m):
        low = (1 - wire.low) if flip_low else wire.low
        section = wire.section_at(s) if s else wire.section
        high = wire.high_at(m) if m else wire.high
        peer = {"section": section, "dp": high * 2 + low}
        return (low * sections + section) * outer + high, peer

    mine = at(0, 0, 0)[0]
    own = pltpu.make_async_copy(columns.at[mine], columns_in.at[mine], own_sem)
    own.start()
    others = [
        (f, s, m) for m in range(outer) for s in range(sections) for f in range(2) if f + s + m
    ][::-1]
    barrier = pltpu.get_barrier_semaphore()
    peers = [at(*o)[1] for o in others] + [wire.to_expert(m) for m in range(1, wire.experts)]
    for peer in peers:
        pl.semaphore_signal(barrier, inc=1, device_id=peer, device_id_type=MESH)
    pl.semaphore_wait(barrier, len(peers))
    masks = wire.expert_masks() + [0]
    exchange = []
    for other in others:
        index, peer = at(*other)
        exchange.append(wire.send(columns.at[index], columns_in.at[mine], peer))
    pairs = [(i, i) for i in range(parts.shape[1])]
    flows = fold_start(wire, parts, near_in, pairs)
    far = {c: fold_near(wire, flows, parts, near_in, far_in, c, index) for c, index in pairs}
    own.wait()
    for copy in exchange:
        copy.wait_recv()
    crossing = {}
    for c in masks:
        index = wire.expert_at(c)
        product = jnp.dot(features[0, index], columns_in[0], preferred_element_type=jnp.float32)
        for p in range(1, 2 * span):
            product = product + jnp.dot(
                features[p, index], columns_in[p], preferred_element_type=jnp.float32
            )
        total[index] = product.astype(jnp.bfloat16)
        if c:
            crossing[c] = wire.send(total.at[index], cross_in.at[c - 1], wire.to_expert(c))
    for c, index in pairs:
        out[index] = fold_far(wire, far[c], near_in, far_in, index)
    for c in crossing:
        crossing[c].wait_recv()
    place = wire.low * span + wire.section * outer + wire.high
    weight_out[place] = added(
        total[wire.expert], *[cross_in[m - 1] for m in range(1, wire.experts)]
    )
    base = wire.low * span
    passed = []
    wide = [
        wire.send(weight_out.at[place], weight_out.at[place], wire.to_high(m))
        for m in range(1, outer)
    ]
    side = [
        wire.send(weight_out.at[place], weight_out.at[place], wire.to_section(m))
        for m in range(1, sections)
    ]
    passed.append(wire.send(weight_out.at[place], weight_out.at[place], wire.to_low()))
    relayed = []
    for m, copy in enumerate(wide, 1):
        copy.wait_recv()
        block = weight_out.at[base + wire.section * outer + wire.high_at(m)]
        relayed += [
            (m, s, wire.send(block, block, wire.to_section(s))) for s in range(1, sections)
        ]
        passed.append(wire.send(block, block, wire.to_low()))
    for s, copy in enumerate(side, 1):
        copy.wait_recv()
        block = weight_out.at[base + wire.section_at(s) * outer + wire.high]
        passed.append(wire.send(block, block, wire.to_low()))
    for m, s, copy in relayed:
        copy.wait_recv()
        block = weight_out.at[base + wire.section_at(s) * outer + wire.high_at(m)]
        passed.append(wire.send(block, block, wire.to_low()))
    settle(wire, passed)


def call(kernel, sizes, ident, copies, operands, outs, scratch=(), extra=()):
    low = lambda shape: jax.ShapeDtypeStruct(shape, jnp.bfloat16)
    return pl.pallas_call(
        functools.partial(kernel, sizes),
        out_shape=[low(s) for s in outs],
        in_specs=[WHOLE] * len(operands),
        out_specs=[WHOLE] * len(outs),
        scratch_shapes=[pltpu.VMEM(s, jnp.bfloat16) for s in scratch]
        + [pltpu.SemaphoreType.DMA((copies,)), pltpu.SemaphoreType.DMA((copies,))]
        + list(extra),
        compiler_params=pltpu.CompilerParams(
            collective_id=ident, has_side_effects=True, vmem_limit_bytes=60 * 1024 * 1024
        ),
    )(*operands)


def expert_kernel(
    sizes, rows, grads, features, gate_hbm, up_hbm, down_hbm, grad_back, back, features_out,
    gathered, gate, up, down, act, gate_grad, up_grad, parts, near_in, far_in, total,
    zs, zr, hs, hr, ls, lr, fls, flr, fhs, fhr, fzs, fzr, ps, pr, weight_sems, own_sems,
):
    wire = Wire(sizes, None, None)
    experts, outer, ways = wire.experts, wire.outer, wire.ways
    capacity, width = rows.shape[1], rows.shape[2]
    hidden_units = gate.shape[1]
    backs = (grad_back, back)
    loads = [
        pltpu.make_async_copy(source.at[0], target, weight_sems.at[i])
        for i, (source, target) in enumerate(((gate_hbm, gate), (up_hbm, up), (down_hbm, down)))
    ]
    own = pltpu.make_async_copy(
        rows.at[wire.expert], gathered.at[wire.dp, wire.expert], own_sems.at[0]
    )
    own.start()
    sections = wire.sections
    span = outer * sections

    def place(low, section, high):
        return (low * sections + section) * outer + high

    def at_masks(s, m):
        return (wire.section_at(s) if s else wire.section), (
            wire.high_at(m) if m else wire.high
        )

    mine = place(wire.low, wire.section, wire.high)
    own_features = pltpu.make_async_copy(features, features_out.at[mine], own_sems.at[1])
    own_features.start()
    for load in loads:
        load.start()
    wire.greet(sections=True)

    def link(source, target, send_sem, recv_sem, peer):
        return pltpu.make_async_remote_copy(
            src_ref=source, dst_ref=target, send_sem=send_sem, recv_sem=recv_sem,
            device_id=peer, device_id_type=MESH,
        )

    def over_expert(mask):
        return link(
            rows.at[wire.expert_at(mask)], gathered.at[wire.dp, wire.expert],
            zs.at[mask], zr.at[mask], wire.to_expert(mask),
        )

    def over_high(m, mask):
        block = gathered.at[wire.dp, wire.expert_at(mask)]
        return link(block, block, hs.at[m - 1, mask], hr.at[m - 1, mask], wire.to_high(m))

    def over_low(m, mask):
        block = gathered.at[wire.dp_at(m) if m else wire.dp, wire.expert_at(mask)]
        return link(block, block, ls.at[m, mask], lr.at[m, mask], wire.to_low())

    def back_low(r, h, mask):
        index = wire.expert_at(mask)
        return link(
            parts.at[r, h * 2 + (1 - wire.low), index], near_in.at[r, h, index],
            fls.at[r, h, mask], flr.at[r, h, mask], wire.to_low(),
        )

    def back_high(r, m, mask):
        index = wire.expert_at(mask)
        return link(
            near_in.at[r, wire.high_at(m), index], far_in.at[r, m - 1, index],
            fhs.at[r, m - 1, mask], fhr.at[r, m - 1, mask], wire.to_high(m),
        )

    def back_expert(r, mask):
        index = wire.expert_at(mask)
        return link(
            total.at[r, index], backs[r].at[wire.expert],
            fzs.at[r, mask], fzr.at[r, mask], wire.to_expert(mask),
        )

    def plane_high(m):
        return link(
            features, features_out.at[mine], ps.at[0, m], pr.at[0, m], wire.to_high(m)
        )

    def plane_side(s, m):
        block = features_out.at[place(wire.low, wire.section, at_masks(0, m)[1])]
        return link(
            block if m else features, block, ps.at[1, s * outer + m], pr.at[1, s * outer + m],
            wire.to_section(s),
        )

    def plane_low(s, m):
        section, high = at_masks(s, m)
        block = features_out.at[place(wire.low, section, high)]
        return link(
            block if s + m else features, block,
            ps.at[2, s * outer + m], pr.at[2, s * outer + m], wire.to_low(),
        )

    def fold_low(r, mask):
        index = wire.expert_at(mask)
        for h in range(outer):
            back_low(r, h, mask).wait_recv()
            near_in[r, h, index] = added(parts[r, h * 2 + wire.low, index], near_in[r, h, index])
        for m in range(1, outer):
            back_high(r, m, mask).start()

    def fold_high(r, mask, position):
        index = wire.expert_at(mask)
        for m in range(1, outer):
            back_high(r, m, mask).wait_recv()
        summed = added(
            near_in[r, wire.high, index], *[far_in[r, m - 1, index] for m in range(1, outer)]
        )

        @pl.when(position == 0)
        def _():
            backs[r][index] = summed

        @pl.when(position > 0)
        def _():
            total[r, index] = summed
            back_expert(r, mask).start()

    tile = 256

    def units(mask):
        index = wire.expert_at(mask)

        @pl.loop(0, hidden_units // tile)
        def _(j):
            columns = pl.ds(pl.multiple_of(j * tile, tile), tile)
            block = gathered[:, index].reshape(ways * capacity, width)
            grad_block = grads[:, index].reshape(ways * capacity, width)
            gate_pre = jnp.dot(block, gate[:, columns], preferred_element_type=jnp.float32)
            up_pre = jnp.dot(block, up[:, columns], preferred_element_type=jnp.float32)
            grad_act = contract_last(grad_block, down[columns, :])
            sigmoid_gate = jax.nn.sigmoid(gate_pre)
            silu = gate_pre * sigmoid_gate
            act[:, columns] = (silu * up_pre).astype(jnp.bfloat16)
            gate_grad[:, columns] = (
                grad_act * up_pre * sigmoid_gate * (1.0 + gate_pre * (1.0 - sigmoid_gate))
            ).astype(jnp.bfloat16)
            up_grad[:, columns] = (grad_act * silu).astype(jnp.bfloat16)

    def grad_products(mask):
        index = wire.expert_at(mask)

        @pl.loop(0, width // tile)
        def _(j):
            columns = pl.ds(pl.multiple_of(j * tile, tile), tile)
            piece = contract_last(gate_grad[...], gate[columns, :]) + contract_last(
                up_grad[...], up[columns, :]
            )
            parts[0, :, index, :, columns] = piece.astype(jnp.bfloat16).reshape(
                ways, capacity, tile
            )

    def out_products(mask):
        index = wire.expert_at(mask)

        @pl.loop(0, width // tile)
        def _(j):
            columns = pl.ds(pl.multiple_of(j * tile, tile), tile)
            piece = jnp.dot(act[...], down[:, columns], preferred_element_type=jnp.float32)
            parts[1, :, index, :, columns] = piece.astype(jnp.bfloat16).reshape(
                ways, capacity, tile
            )

    for step in range(1, experts):
        over_expert(experts - step).start()
    own.wait()
    own_features.wait()
    for s in range(1, sections):
        plane_side(s, 0).start()
    plane_low(0, 0).start()

    def mask_of(position):
        return lax.rem(experts - position, experts)

    @pl.loop(0, experts + 2)
    def _(step):
        incoming, current, leaving = step < experts, step >= 1, step >= 2
        now, before, last = mask_of(step), mask_of(step - 1), mask_of(step - 2)

        @pl.when(incoming)
        def _():
            @pl.when(step > 0)
            def _():
                over_expert(now).wait_recv()

            for m in range(1, outer):
                over_high(m, now).start()
            over_low(0, now).start()

        @pl.when(leaving)
        def _():
            fold_low(1, last)

        @pl.when(step == 1)
        def _():
            for load in loads:
                load.wait()

        busy = current & (step <= experts)

        @pl.when(busy)
        def _():
            for m in range(outer):
                over_low(m, before).wait_recv()
            units(before)
            grad_products(before)
            for h in range(outer):
                back_low(0, h, before).start()

        @pl.when(incoming)
        def _():
            for m in range(1, outer):
                over_high(m, now).wait_recv()
                over_low(m, now).start()

        @pl.when(step == 0)
        def _():
            for m in range(1, outer):
                plane_high(m).start()

        @pl.when(step == 1)
        def _():
            for m in range(1, outer):
                plane_high(m).wait_recv()
                for s in range(1, sections):
                    plane_side(s, m).start()
                plane_low(0, m).start()

        @pl.when(step == 2)
        def _():
            for s in range(1, sections):
                for m in range(outer):
                    plane_side(s, m).wait_recv()
                    plane_low(s, m).start()

        @pl.when(leaving)
        def _():
            fold_high(0, last, step - 2)

        @pl.when(busy)
        def _():
            out_products(before)
            fold_low(0, before)
            for h in range(outer):
                back_low(1, h, before).start()

        @pl.when(leaving)
        def _():
            fold_high(1, last, step - 2)

    for m in range(1, outer):
        plane_high(m).wait_send()
    for s in range(sections):
        for m in range(outer):
            if s:
                plane_side(s, m).wait_send()
            plane_low(s, m).wait()
    for mask in range(experts):
        for r in range(2):
            if mask:
                back_expert(r, mask).wait()
            for h in range(outer):
                back_low(r, h, mask).wait_send()
            for m in range(1, outer):
                back_high(r, m, mask).wait_send()
        if mask:
            over_expert(mask).wait_send()
        for m in range(1, outer):
            over_high(m, mask).wait_send()
        for m in range(outer):
            over_low(m, mask).wait_send()


def run_experts(sizes, ident, rows, grads, features, gate_weight, up_weight, down_weight):
    sections, experts, ways = sizes
    outer = ways // 2
    span = max(outer - 1, 1)
    buckets = rows.shape
    count = ways * buckets[1]
    units = gate_weight.shape[2]
    anywhere = pl.BlockSpec(memory_space=pl.ANY)
    low = lambda *shape: pltpu.VMEM(shape, jnp.bfloat16)
    sems = []
    for shape in (
        (experts,),
        (span, experts),
        (outer, experts),
        (2, outer, experts),
        (2, span, experts),
        (2, experts),
        (3, sections * outer),
    ):
        sems += [pltpu.SemaphoreType.DMA(shape)] * 2
    return pl.pallas_call(
        functools.partial(expert_kernel, sizes),
        out_shape=[jax.ShapeDtypeStruct(buckets, jnp.bfloat16)] * 2
        + [jax.ShapeDtypeStruct((ways * sections,) + features.shape, jnp.bfloat16)],
        in_specs=[WHOLE, WHOLE, WHOLE, anywhere, anywhere, anywhere],
        out_specs=[WHOLE, WHOLE, WHOLE],
        scratch_shapes=[
            low(ways, *buckets),
            low(*gate_weight.shape[1:]),
            low(*up_weight.shape[1:]),
            low(*down_weight.shape[1:]),
            low(count, units),
            low(count, units),
            low(count, units),
            low(2, ways, *buckets),
            low(2, outer, *buckets),
            low(2, span, *buckets),
            low(2, *buckets),
        ]
        + sems
        + [pltpu.SemaphoreType.DMA((3,)), pltpu.SemaphoreType.DMA((2,))],
        compiler_params=pltpu.CompilerParams(
            collective_id=ident, has_side_effects=True, vmem_limit_bytes=62 * 1024 * 1024
        ),
    )(rows, grads, features, gate_weight, up_weight, down_weight)


def shards(
    residual,
    queries,
    attn_keys,
    attn_values,
    out_weight,
    norm_gain,
    gate_weight,
    up_weight,
    down_weight,
    expert_ids,
    out_grad,
):
    tokens_here = residual.shape[0]
    experts = lax.axis_size("expert")
    data_ways = lax.axis_size("dp")
    capacity = max(tokens_here // 8, 2 * tokens_here // experts)
    inv_root = 1.0 / math.sqrt(HEAD)
    sections = lax.axis_size("section")
    sizes = (sections, experts, data_ways)
    outer = data_ways // 2
    expert_of = expert_ids[:, 0]
    onehot = (expert_of[:, None] == jnp.arange(experts, dtype=jnp.int32)[None, :]).astype(
        jnp.bfloat16
    )
    row_iota = jnp.arange(tokens_here, dtype=jnp.int32)
    earlier_mask = (row_iota[:, None] > row_iota[None, :]).astype(jnp.bfloat16)
    earlier = jnp.dot(earlier_mask, onehot, preferred_element_type=jnp.float32)
    rank_index = jnp.sum(earlier * onehot.astype(jnp.float32), axis=1).astype(jnp.int32)
    slot_index = expert_of * capacity + rank_index
    slot_iota = jnp.arange(experts * capacity, dtype=jnp.int32)
    placing = (slot_iota[:, None] == slot_index[None, :]).astype(jnp.bfloat16)
    buckets = (experts, capacity, D)
    spread_shape = (data_ways,) + buckets
    grad_buffer = jnp.dot(placing, out_grad).reshape(buckets)
    weight_rows = out_weight.shape[0]
    quarter = data_ways * sections
    keys_all, values_all, full_out, grad_gathered = call(
        opening_kernel,
        sizes,
        0,
        4 * outer + experts * (1 + 2 * outer) + experts * (2 + 2 * data_ways * sections),
        (
            attn_keys,
            attn_values,
            out_weight.reshape(quarter, weight_rows // quarter, D),
            grad_buffer,
        ),
        (
            (data_ways,) + attn_keys.shape,
            (data_ways,) + attn_values.shape,
            (experts, quarter, weight_rows // quarter, D),
            spread_shape,
        ),
        extra=(pltpu.SemaphoreType.DMA((4,)),),
    )
    full_out = full_out.reshape(A, D)
    query_heads = queries.reshape(tokens_here, HEADS, HEAD)
    key_heads = keys_all.reshape(-1, HEADS, HEAD)
    value_heads = values_all.reshape(-1, HEADS, HEAD)
    scores = (
        jnp.einsum("thd,shd->hts", query_heads, key_heads, preferred_element_type=jnp.float32)
        * inv_root
    )
    row_peak = jnp.max(scores, axis=-1, keepdims=True)
    exp_scores = jnp.exp(scores - row_peak)
    attn_probs = exp_scores / jnp.sum(exp_scores, axis=-1, keepdims=True)
    probs_low = attn_probs.astype(jnp.bfloat16)
    attended = (
        jnp.einsum("hts,shd->thd", probs_low, value_heads, preferred_element_type=jnp.float32)
        .reshape(tokens_here, A)
        .astype(jnp.bfloat16)
    )
    hidden = residual.astype(jnp.float32) + jnp.dot(
        attended, full_out, preferred_element_type=jnp.float32
    )
    inv_rms = lax.rsqrt(jnp.mean(hidden * hidden, axis=-1, keepdims=True) + epsilon)
    unit_rows = hidden * inv_rms
    normed = (unit_rows * norm_gain).astype(jnp.bfloat16)
    send_buffer = jnp.dot(placing, normed).reshape(buckets)
    grad_returned, returned, features_all = run_experts(
        sizes, 1, send_buffer, grad_gathered, attended.T, gate_weight, up_weight, down_weight
    )
    expert_back = contract_first(placing, returned.reshape(experts * capacity, D))
    layer_out = (hidden + expert_back.astype(jnp.float32)).astype(jnp.bfloat16)
    grad_normed = contract_first(placing, grad_returned.reshape(experts * capacity, D))
    scaled = grad_normed * norm_gain
    resid_grad = (
        out_grad.astype(jnp.float32)
        + inv_rms * (scaled - unit_rows * jnp.mean(scaled * unit_rows, axis=-1, keepdims=True))
    ).astype(jnp.bfloat16)
    ways = data_ways * sections
    width = D // ways
    columns = resid_grad.reshape(tokens_here, ways, width).transpose(1, 0, 2)
    grad_attended = contract_last(resid_grad, full_out).astype(jnp.bfloat16)
    grad_heads = grad_attended.reshape(tokens_here, HEADS, HEAD)
    grad_probs = jnp.einsum(
        "thd,shd->hts", grad_heads, value_heads, preferred_element_type=jnp.float32
    )
    row_delta = jnp.sum(attn_probs * grad_probs, axis=-1, keepdims=True)
    grad_scores = (attn_probs * (grad_probs - row_delta)).astype(jnp.bfloat16)
    query_grad = (
        (
            jnp.einsum("hts,shd->thd", grad_scores, key_heads, preferred_element_type=jnp.float32)
            * inv_root
        )
        .reshape(tokens_here, A)
        .astype(jnp.bfloat16)
    )
    key_part = (
        jnp.einsum("hts,thd->shd", grad_scores, query_heads, preferred_element_type=jnp.float32)
        * inv_root
    )
    value_part = jnp.einsum(
        "hts,thd->shd", probs_low, grad_heads, preferred_element_type=jnp.float32
    )
    pair_parts = jnp.stack(
        [
            key_part.reshape(data_ways, tokens_here, A),
            value_part.reshape(data_ways, tokens_here, A),
        ],
        axis=1,
    ).astype(jnp.bfloat16)
    pair = (2, tokens_here, A)
    block = (weight_rows, width)
    key_value, weight_parts = call(
        closing_kernel,
        sizes,
        2,
        4 * outer + experts + 4 * ways,
        (
            pair_parts,
            features_all.reshape(ways, experts, weight_rows, tokens_here),
            columns,
        ),
        (pair, (ways,) + block),
        (
            (outer,) + pair,
            (max(outer - 1, 1),) + pair,
            columns.shape,
            (experts,) + block,
            (experts - 1,) + block,
        ),
        extra=(pltpu.SemaphoreType.DMA,),
    )
    key_grad, value_grad = key_value[0], key_value[1]
    weight_grad = weight_parts.transpose(1, 0, 2).reshape(weight_rows, D).astype(jnp.float32)
    return (layer_out, resid_grad, query_grad, key_grad, value_grad, weight_grad)


def solution(mesh):
    return jax.shard_map(
        shards,
        mesh=mesh,
        in_specs=(
            P(("section", "expert", "dp"), None),
            P(("section", "expert", "dp"), None),
            P(("section", "expert", "dp"), None),
            P(("section", "expert", "dp"), None),
            P("expert", None),
            P(),
            P("expert", None, "dp"),
            P("expert", None, "dp"),
            P("expert", "dp", None),
            P(("section", "expert", "dp"), None),
            P(("section", "expert", "dp"), None),
        ),
        out_specs=(
            P(("section", "expert", "dp"), None),
            P(("section", "expert", "dp"), None),
            P(("section", "expert", "dp"), None),
            P(("section", "expert", "dp"), None),
            P(("section", "expert", "dp"), None),
            P("expert", None),
        ),
        check_vma=False,
    )
```

```python
import functools
import math

import jax
import jax.numpy as jnp
from jax import lax
from jax.experimental import pallas as pl
from jax.experimental.pallas import tpu as pltpu
from jax.sharding import PartitionSpec as P

D = 2048
HEADS = 8
HEAD = 128
A = 1024
FF = 4096


epsilon = 1e-06


def contract_last(left_side, right_side):
    return lax.dot_general(
        left_side, right_side, (((1,), (1,)), ((), ())), preferred_element_type=jnp.float32
    )


def contract_first(left_side, right_side):
    return lax.dot_general(
        left_side, right_side, (((0,), (0,)), ((), ())), preferred_element_type=jnp.float32
    )


MESH = pl.DeviceIdType.MESH
WHOLE = pl.BlockSpec(memory_space=pltpu.VMEM)


def flip(index, mask, size):
    total, bit = 0, 1
    while bit < size:
        total = total + bit * lax.rem(lax.div(index, bit) + (mask // bit), 2)
        bit *= 2
    return total


class Wire:
    def __init__(self, sizes, send_sems, recv_sems):
        self.sections, self.experts, self.ways = sizes
        self.outer = self.ways // 2
        self.section = lax.axis_index("section")
        self.expert = lax.axis_index("expert")
        self.dp = lax.axis_index("dp")
        self.low = lax.rem(self.dp, 2)
        self.high = lax.div(self.dp, 2)
        self.send_sems, self.recv_sems = send_sems, recv_sems
        self.started = []

    def send(self, source, target, peer):
        slot = len(self.started)
        copy = pltpu.make_async_remote_copy(
            src_ref=source,
            dst_ref=target,
            send_sem=self.send_sems.at[slot],
            recv_sem=self.recv_sems.at[slot],
            device_id=peer,
            device_id_type=MESH,
        )
        copy.start()
        self.started.append(copy)
        return copy

    def finish(self):
        for copy in self.started:
            copy.wait_send()

    def expert_at(self, mask):
        return flip(self.expert, mask, self.experts)

    def high_at(self, mask):
        return flip(self.high, mask, self.outer)

    def section_at(self, mask):
        return flip(self.section, mask, self.sections)

    def dp_at(self, mask):
        return self.high_at(mask) * 2 + self.low

    def to_expert(self, mask):
        return {"expert": self.expert_at(mask)}

    def to_high(self, mask):
        return {"dp": self.dp_at(mask)}

    def to_section(self, mask):
        return {"section": self.section_at(mask)}

    def to_low(self):
        return {"dp": self.high * 2 + (1 - self.low)}

    def expert_masks(self):
        half = self.experts // 2
        return list(range(half, self.experts)) + list(range(1, half))

    def greet(self, experts=True, sections=False):
        peers = [self.to_low()] + [self.to_high(m) for m in range(1, self.outer)]
        if experts:
            peers += [self.to_expert(m) for m in range(1, self.experts)]
        if sections:
            peers += [self.to_section(m) for m in range(1, self.sections)]
        barrier = pltpu.get_barrier_semaphore()
        for peer in peers:
            pl.semaphore_signal(barrier, inc=1, device_id=peer, device_id_type=MESH)
        pl.semaphore_wait(barrier, len(peers))


def added(first, *others):
    total = first.astype(jnp.float32)
    for other in others:
        total = total + other.astype(jnp.float32)
    return total.astype(jnp.bfloat16)


def gather_start(wire, block, out):
    wide = [wire.send(block, out.at[wire.dp], wire.to_high(m)) for m in range(1, wire.outer)]
    near = wire.send(block, out.at[wire.dp], wire.to_low())
    return wide, near


def gather_end(wire, flow, out):
    wide, near = flow
    passed = [near]
    for m, copy in enumerate(wide, 1):
        copy.wait_recv()
        block = out.at[wire.dp_at(m)]
        passed.append(wire.send(block, block, wire.to_low()))
    return passed


def cross(wire, source, out):
    return {
        m: wire.send(source.at[wire.expert_at(m)], out.at[wire.dp, wire.expert], wire.to_expert(m))
        for m in wire.expert_masks()
    }


def spread_own(wire, source, out):
    block, target = source.at[wire.expert], out.at[wire.dp, wire.expert]
    wide = [wire.send(block, target, wire.to_high(m)) for m in range(1, wire.outer)]
    return wide, wire.send(block, target, wire.to_low())


def spread(wire, out, crossing, first):
    passed = [first[1]]
    held = (0, first[0])

    def hand_over(mask, wide):
        for m, copy in enumerate(wide, 1):
            copy.wait_recv()
            block = out.at[wire.dp_at(m), wire.expert_at(mask)]
            passed.append(wire.send(block, block, wire.to_low()))

    for mask in wire.expert_masks():
        block = out.at[wire.dp, wire.expert_at(mask)]
        crossing[mask].wait_recv()
        wide = [wire.send(block, block, wire.to_high(m)) for m in range(1, wire.outer)]
        passed.append(wire.send(block, block, wire.to_low()))
        hand_over(*held)
        held = (mask, wide)
    hand_over(*held)
    return passed


def settle(wire, passed):
    for copy in passed:
        copy.wait_recv()
    wire.finish()


def opening_kernel(
    sizes, keys, values, weight, rows, keys_out, values_out, weight_out, out,
    send_sems, recv_sems, own_sems,
):
    wire = Wire(sizes, send_sems, recv_sems)
    local = [
        pltpu.make_async_copy(source, target, own_sems.at[i])
        for i, (source, target) in enumerate(
            (
                (keys, keys_out.at[wire.dp]),
                (values, values_out.at[wire.dp]),
                (weight, weight_out.at[wire.expert]),
                (rows.at[wire.expert], out.at[wire.dp, wire.expert]),
            )
        )
    ]
    for copy in local:
        copy.start()
    wire.greet(sections=True)
    key_flow = gather_start(wire, keys, keys_out)
    value_flow = gather_start(wire, values, values_out)
    outer, sections = wire.outer, wire.sections

    def piece(mask, section, high):
        return weight_out.at[wire.expert_at(mask), (section * 2 + wire.low) * outer + high]

    part = (wire.section * 2 + wire.low) * outer + wire.high
    pieces = {
        m: wire.send(weight.at[part], weight_out.at[wire.expert, part], wire.to_expert(m))
        for m in wire.expert_masks()
    }
    crossing = cross(wire, rows, out)
    passed = gather_end(wire, key_flow, keys_out) + gather_end(wire, value_flow, values_out)
    wides, sides = [], []
    for mask in wire.expert_masks():
        pieces[mask].wait_recv()
        block = piece(mask, wire.section, wire.high)
        for m in range(1, outer):
            wides.append((mask, m, wire.send(block, block, wire.to_high(m))))
        for s in range(1, sections):
            sides.append((mask, 0, s, wire.send(block, block, wire.to_section(s))))
        passed.append(wire.send(block, block, wire.to_low()))
    first = spread_own(wire, rows, out)
    for mask, m, copy in wides:
        copy.wait_recv()
        block = piece(mask, wire.section, wire.high_at(m))
        for s in range(1, sections):
            sides.append((mask, m, s, wire.send(block, block, wire.to_section(s))))
        passed.append(wire.send(block, block, wire.to_low()))
    passed += spread(wire, out, crossing, first)
    for mask, m, s, copy in sides:
        copy.wait_recv()
        block = piece(mask, wire.section_at(s), wire.high_at(m) if m else wire.high)
        passed.append(wire.send(block, block, wire.to_low()))
    settle(wire, passed)
    for copy in local:
        copy.wait()


def fold_start(wire, parts, near_in, chunks):
    return {
        c: [
            wire.send(
                parts.at[h * 2 + (1 - wire.low), index],
                near_in.at[h, index],
                wire.to_low(),
            )
            for h in range(wire.outer)
        ]
        for c, index in chunks
    }


def fold_near(wire, flows, parts, near_in, far_in, c, index):
    for copy in flows[c]:
        copy.wait_recv()
    for h in range(wire.outer):
        near_in[h, index] = added(parts[h * 2 + wire.low, index], near_in[h, index])
    return [
        wire.send(near_in.at[wire.high_at(m), index], far_in.at[m - 1, index], wire.to_high(m))
        for m in range(1, wire.outer)
    ]


def fold_far(wire, far, near_in, far_in, index):
    for copy in far:
        copy.wait_recv()
    return added(
        near_in[wire.high, index], *[far_in[m - 1, index] for m in range(1, wire.outer)]
    )


def closing_kernel(
    sizes, parts, features, columns, out, weight_out,
    near_in, far_in, columns_in, total, cross_in, send_sems, recv_sems, own_sem,
):
    wire = Wire(sizes, send_sems, recv_sems)
    outer, sections = wire.outer, wire.sections
    span = outer * sections

    def at(flip_low, s, m):
        low = (1 - wire.low) if flip_low else wire.low
        section = wire.section_at(s) if s else wire.section
        high = wire.high_at(m) if m else wire.high
        peer = {"section": section, "dp": high * 2 + low}
        return (low * sections + section) * outer + high, peer

    mine = at(0, 0, 0)[0]
    own = pltpu.make_async_copy(columns.at[mine], columns_in.at[mine], own_sem)
    own.start()
    others = [
        (f, s, m) for m in range(outer) for s in range(sections) for f in range(2) if f + s + m
    ][::-1]
    barrier = pltpu.get_barrier_semaphore()
    peers = [at(*o)[1] for o in others] + [wire.to_expert(m) for m in range(1, wire.experts)]
    for peer in peers:
        pl.semaphore_signal(barrier, inc=1, device_id=peer, device_id_type=MESH)
    pl.semaphore_wait(barrier, len(peers))
    masks = wire.expert_masks() + [0]
    exchange = []
    for other in others:
        index, peer = at(*other)
        exchange.append(wire.send(columns.at[index], columns_in.at[mine], peer))
    pairs = [(i, i) for i in range(parts.shape[1])]
    flows = fold_start(wire, parts, near_in, pairs)
    far = {c: fold_near(wire, flows, parts, near_in, far_in, c, index) for c, index in pairs}
    own.wait()
    for copy in exchange:
        copy.wait_recv()
    crossing = {}
    for c in masks:
        index = wire.expert_at(c)
        product = jnp.dot(features[0, index], columns_in[0], preferred_element_type=jnp.float32)
        for p in range(1, 2 * span):
            product = product + jnp.dot(
                features[p, index], columns_in[p], preferred_element_type=jnp.float32
            )
        total[index] = product.astype(jnp.bfloat16)
        if c:
            crossing[c] = wire.send(total.at[index], cross_in.at[c - 1], wire.to_expert(c))
    for c, index in pairs:
        out[index] = fold_far(wire, far[c], near_in, far_in, index)
    for c in crossing:
        crossing[c].wait_recv()
    place = wire.low * span + wire.section * outer + wire.high
    weight_out[place] = added(
        total[wire.expert], *[cross_in[m - 1] for m in range(1, wire.experts)]
    )
    base = wire.low * span
    passed = []
    wide = [
        wire.send(weight_out.at[place], weight_out.at[place], wire.to_high(m))
        for m in range(1, outer)
    ]
    side = [
        wire.send(weight_out.at[place], weight_out.at[place], wire.to_section(m))
        for m in range(1, sections)
    ]
    passed.append(wire.send(weight_out.at[place], weight_out.at[place], wire.to_low()))
    relayed = []
    for m, copy in enumerate(wide, 1):
        copy.wait_recv()
        block = weight_out.at[base + wire.section * outer + wire.high_at(m)]
        relayed += [
            (m, s, wire.send(block, block, wire.to_section(s))) for s in range(1, sections)
        ]
        passed.append(wire.send(block, block, wire.to_low()))
    for s, copy in enumerate(side, 1):
        copy.wait_recv()
        block = weight_out.at[base + wire.section_at(s) * outer + wire.high]
        passed.append(wire.send(block, block, wire.to_low()))
    for m, s, copy in relayed:
        copy.wait_recv()
        block = weight_out.at[base + wire.section_at(s) * outer + wire.high_at(m)]
        passed.append(wire.send(block, block, wire.to_low()))
    settle(wire, passed)


def call(kernel, sizes, ident, copies, operands, outs, scratch=(), extra=()):
    low = lambda shape: jax.ShapeDtypeStruct(shape, jnp.bfloat16)
    return pl.pallas_call(
        functools.partial(kernel, sizes),
        out_shape=[low(s) for s in outs],
        in_specs=[WHOLE] * len(operands),
        out_specs=[WHOLE] * len(outs),
        scratch_shapes=[pltpu.VMEM(s, jnp.bfloat16) for s in scratch]
        + [pltpu.SemaphoreType.DMA((copies,)), pltpu.SemaphoreType.DMA((copies,))]
        + list(extra),
        compiler_params=pltpu.CompilerParams(
            collective_id=ident, has_side_effects=True, vmem_limit_bytes=60 * 1024 * 1024
        ),
    )(*operands)


def expert_kernel(
    sizes, rows, grads, features, gate_hbm, up_hbm, down_hbm, grad_back, back, features_out,
    gathered, gate, up, down, act, gate_grad, up_grad, parts, near_in, far_in, total,
    zs, zr, hs, hr, ls, lr, fls, flr, fhs, fhr, fzs, fzr, ps, pr, weight_sems, own_sems,
):
    wire = Wire(sizes, None, None)
    experts, outer, ways = wire.experts, wire.outer, wire.ways
    capacity, width = rows.shape[1], rows.shape[2]
    hidden_units = gate.shape[1]
    backs = (grad_back, back)
    loads = [
        pltpu.make_async_copy(source.at[0], target, weight_sems.at[i])
        for i, (source, target) in enumerate(((gate_hbm, gate), (up_hbm, up), (down_hbm, down)))
    ]
    own = pltpu.make_async_copy(
        rows.at[wire.expert], gathered.at[wire.dp, wire.expert], own_sems.at[0]
    )
    own.start()
    sections = wire.sections
    span = outer * sections

    def place(low, section, high):
        return (low * sections + section) * outer + high

    def at_masks(s, m):
        return (wire.section_at(s) if s else wire.section), (
            wire.high_at(m) if m else wire.high
        )

    mine = place(wire.low, wire.section, wire.high)
    own_features = pltpu.make_async_copy(features, features_out.at[mine], own_sems.at[1])
    own_features.start()
    for load in loads:
        load.start()
    wire.greet(sections=True)

    def link(source, target, send_sem, recv_sem, peer):
        return pltpu.make_async_remote_copy(
            src_ref=source, dst_ref=target, send_sem=send_sem, recv_sem=recv_sem,
            device_id=peer, device_id_type=MESH,
        )

    def over_expert(mask):
        return link(
            rows.at[wire.expert_at(mask)], gathered.at[wire.dp, wire.expert],
            zs.at[mask], zr.at[mask], wire.to_expert(mask),
        )

    def over_high(m, mask):
        block = gathered.at[wire.dp, wire.expert_at(mask)]
        return link(block, block, hs.at[m - 1, mask], hr.at[m - 1, mask], wire.to_high(m))

    def over_low(m, mask):
        block = gathered.at[wire.dp_at(m) if m else wire.dp, wire.expert_at(mask)]
        return link(block, block, ls.at[m, mask], lr.at[m, mask], wire.to_low())

    def back_low(r, h, mask):
        index = wire.expert_at(mask)
        return link(
            parts.at[r, h * 2 + (1 - wire.low), index], near_in.at[r, h, index],
            fls.at[r, h, mask], flr.at[r, h, mask], wire.to_low(),
        )

    def back_high(r, m, mask):
        index = wire.expert_at(mask)
        return link(
            near_in.at[r, wire.high_at(m), index], far_in.at[r, m - 1, index],
            fhs.at[r, m - 1, mask], fhr.at[r, m - 1, mask], wire.to_high(m),
        )

    def back_expert(r, mask):
        index = wire.expert_at(mask)
        return link(
            total.at[r, index], backs[r].at[wire.expert],
            fzs.at[r, mask], fzr.at[r, mask], wire.to_expert(mask),
        )

    def plane_high(m):
        return link(
            features, features_out.at[mine], ps.at[0, m], pr.at[0, m], wire.to_high(m)
        )

    def plane_side(s, m):
        block = features_out.at[place(wire.low, wire.section, at_masks(0, m)[1])]
        return link(
            block if m else features, block, ps.at[1, s * outer + m], pr.at[1, s * outer + m],
            wire.to_section(s),
        )

    def plane_low(s, m):
        section, high = at_masks(s, m)
        block = features_out.at[place(wire.low, section, high)]
        return link(
            block if s + m else features, block,
            ps.at[2, s * outer + m], pr.at[2, s * outer + m], wire.to_low(),
        )

    def fold_low(r, mask):
        index = wire.expert_at(mask)
        for h in range(outer):
            back_low(r, h, mask).wait_recv()
            near_in[r, h, index] = added(parts[r, h * 2 + wire.low, index], near_in[r, h, index])
        for m in range(1, outer):
            back_high(r, m, mask).start()

    def fold_high(r, mask, position):
        index = wire.expert_at(mask)
        for m in range(1, outer):
            back_high(r, m, mask).wait_recv()
        summed = added(
            near_in[r, wire.high, index], *[far_in[r, m - 1, index] for m in range(1, outer)]
        )

        @pl.when(position == 0)
        def _():
            backs[r][index] = summed

        @pl.when(position > 0)
        def _():
            total[r, index] = summed
            back_expert(r, mask).start()

    tile = 256

    def units(mask):
        index = wire.expert_at(mask)

        @pl.loop(0, hidden_units // tile)
        def _(j):
            columns = pl.ds(pl.multiple_of(j * tile, tile), tile)
            block = gathered[:, index].reshape(ways * capacity, width)
            grad_block = grads[:, index].reshape(ways * capacity, width)
            gate_pre = jnp.dot(block, gate[:, columns], preferred_element_type=jnp.float32)
            up_pre = jnp.dot(block, up[:, columns], preferred_element_type=jnp.float32)
            grad_act = contract_last(grad_block, down[columns, :])
            sigmoid_gate = jax.nn.sigmoid(gate_pre)
            silu = gate_pre * sigmoid_gate
            act[:, columns] = (silu * up_pre).astype(jnp.bfloat16)
            gate_grad[:, columns] = (
                grad_act * up_pre * sigmoid_gate * (1.0 + gate_pre * (1.0 - sigmoid_gate))
            ).astype(jnp.bfloat16)
            up_grad[:, columns] = (grad_act * silu).astype(jnp.bfloat16)

    def grad_products(mask):
        index = wire.expert_at(mask)

        @pl.loop(0, width // tile)
        def _(j):
            columns = pl.ds(pl.multiple_of(j * tile, tile), tile)
            piece = contract_last(gate_grad[...], gate[columns, :]) + contract_last(
                up_grad[...], up[columns, :]
            )
            parts[0, :, index, :, columns] = piece.astype(jnp.bfloat16).reshape(
                ways, capacity, tile
            )

    def out_products(mask):
        index = wire.expert_at(mask)

        @pl.loop(0, width // tile)
        def _(j):
            columns = pl.ds(pl.multiple_of(j * tile, tile), tile)
            piece = jnp.dot(act[...], down[:, columns], preferred_element_type=jnp.float32)
            parts[1, :, index, :, columns] = piece.astype(jnp.bfloat16).reshape(
                ways, capacity, tile
            )

    for step in range(1, experts):
        over_expert(experts - step).start()
    own.wait()
    own_features.wait()
    for s in range(1, sections):
        plane_side(s, 0).start()
    plane_low(0, 0).start()

    def mask_of(position):
        return lax.rem(experts - position, experts)

    @pl.loop(0, experts + 2)
    def _(step):
        incoming, current, leaving = step < experts, step >= 1, step >= 2
        now, before, last = mask_of(step), mask_of(step - 1), mask_of(step - 2)

        @pl.when(leaving)
        def _():
            fold_low(1, last)

        @pl.when(step == 1)
        def _():
            for load in loads:
                load.wait()

        busy = current & (step <= experts)

        @pl.when(busy)
        def _():
            for m in range(outer):
                over_low(m, before).wait_recv()
            units(before)

        @pl.when(incoming)
        def _():
            @pl.when(step > 0)
            def _():
                over_expert(now).wait_recv()

            for m in range(1, outer):
                over_high(m, now).start()
            over_low(0, now).start()

        @pl.when(busy)
        def _():
            grad_products(before)
            for h in range(outer):
                back_low(0, h, before).start()

        @pl.when(incoming)
        def _():
            for m in range(1, outer):
                over_high(m, now).wait_recv()
                over_low(m, now).start()

        @pl.when(step == 0)
        def _():
            for m in range(1, outer):
                plane_high(m).start()

        @pl.when(step == 1)
        def _():
            for m in range(1, outer):
                plane_high(m).wait_recv()
                for s in range(1, sections):
                    plane_side(s, m).start()
                plane_low(0, m).start()

        @pl.when(step == 2)
        def _():
            for s in range(1, sections):
                for m in range(outer):
                    plane_side(s, m).wait_recv()
                    plane_low(s, m).start()

        @pl.when(leaving)
        def _():
            fold_high(0, last, step - 2)

        @pl.when(busy)
        def _():
            out_products(before)
            fold_low(0, before)
            for h in range(outer):
                back_low(1, h, before).start()

        @pl.when(leaving)
        def _():
            fold_high(1, last, step - 2)

    for m in range(1, outer):
        plane_high(m).wait_send()
    for s in range(sections):
        for m in range(outer):
            if s:
                plane_side(s, m).wait_send()
            plane_low(s, m).wait()
    for mask in range(experts):
        for r in range(2):
            if mask:
                back_expert(r, mask).wait()
            for h in range(outer):
                back_low(r, h, mask).wait_send()
            for m in range(1, outer):
                back_high(r, m, mask).wait_send()
        if mask:
            over_expert(mask).wait_send()
        for m in range(1, outer):
            over_high(m, mask).wait_send()
        for m in range(outer):
            over_low(m, mask).wait_send()


def run_experts(sizes, ident, rows, grads, features, gate_weight, up_weight, down_weight):
    sections, experts, ways = sizes
    outer = ways // 2
    span = max(outer - 1, 1)
    buckets = rows.shape
    count = ways * buckets[1]
    units = gate_weight.shape[2]
    anywhere = pl.BlockSpec(memory_space=pl.ANY)
    low = lambda *shape: pltpu.VMEM(shape, jnp.bfloat16)
    sems = []
    for shape in (
        (experts,),
        (span, experts),
        (outer, experts),
        (2, outer, experts),
        (2, span, experts),
        (2, experts),
        (3, sections * outer),
    ):
        sems += [pltpu.SemaphoreType.DMA(shape)] * 2
    return pl.pallas_call(
        functools.partial(expert_kernel, sizes),
        out_shape=[jax.ShapeDtypeStruct(buckets, jnp.bfloat16)] * 2
        + [jax.ShapeDtypeStruct((ways * sections,) + features.shape, jnp.bfloat16)],
        in_specs=[WHOLE, WHOLE, WHOLE, anywhere, anywhere, anywhere],
        out_specs=[WHOLE, WHOLE, WHOLE],
        scratch_shapes=[
            low(ways, *buckets),
            low(*gate_weight.shape[1:]),
            low(*up_weight.shape[1:]),
            low(*down_weight.shape[1:]),
            low(count, units),
            low(count, units),
            low(count, units),
            low(2, ways, *buckets),
            low(2, outer, *buckets),
            low(2, span, *buckets),
            low(2, *buckets),
        ]
        + sems
        + [pltpu.SemaphoreType.DMA((3,)), pltpu.SemaphoreType.DMA((2,))],
        compiler_params=pltpu.CompilerParams(
            collective_id=ident, has_side_effects=True, vmem_limit_bytes=62 * 1024 * 1024
        ),
    )(rows, grads, features, gate_weight, up_weight, down_weight)


def shards(
    residual,
    queries,
    attn_keys,
    attn_values,
    out_weight,
    norm_gain,
    gate_weight,
    up_weight,
    down_weight,
    expert_ids,
    out_grad,
):
    tokens_here = residual.shape[0]
    experts = lax.axis_size("expert")
    data_ways = lax.axis_size("dp")
    capacity = max(tokens_here // 8, 2 * tokens_here // experts)
    inv_root = 1.0 / math.sqrt(HEAD)
    sections = lax.axis_size("section")
    sizes = (sections, experts, data_ways)
    outer = data_ways // 2
    expert_of = expert_ids[:, 0]
    onehot = (expert_of[:, None] == jnp.arange(experts, dtype=jnp.int32)[None, :]).astype(
        jnp.bfloat16
    )
    row_iota = jnp.arange(tokens_here, dtype=jnp.int32)
    earlier_mask = (row_iota[:, None] > row_iota[None, :]).astype(jnp.bfloat16)
    earlier = jnp.dot(earlier_mask, onehot, preferred_element_type=jnp.float32)
    rank_index = jnp.sum(earlier * onehot.astype(jnp.float32), axis=1).astype(jnp.int32)
    slot_index = expert_of * capacity + rank_index
    slot_iota = jnp.arange(experts * capacity, dtype=jnp.int32)
    placing = (slot_iota[:, None] == slot_index[None, :]).astype(jnp.bfloat16)
    buckets = (experts, capacity, D)
    spread_shape = (data_ways,) + buckets
    grad_buffer = jnp.dot(placing, out_grad).reshape(buckets)
    weight_rows = out_weight.shape[0]
    quarter = data_ways * sections
    keys_all, values_all, full_out, grad_gathered = call(
        opening_kernel,
        sizes,
        0,
        4 * outer + experts * (1 + 2 * outer) + experts * (2 + 2 * data_ways * sections),
        (
            attn_keys,
            attn_values,
            out_weight.reshape(quarter, weight_rows // quarter, D),
            grad_buffer,
        ),
        (
            (data_ways,) + attn_keys.shape,
            (data_ways,) + attn_values.shape,
            (experts, quarter, weight_rows // quarter, D),
            spread_shape,
        ),
        extra=(pltpu.SemaphoreType.DMA((4,)),),
    )
    full_out = full_out.reshape(A, D)
    query_heads = queries.reshape(tokens_here, HEADS, HEAD)
    key_heads = keys_all.reshape(-1, HEADS, HEAD)
    value_heads = values_all.reshape(-1, HEADS, HEAD)
    scores = (
        jnp.einsum("thd,shd->hts", query_heads, key_heads, preferred_element_type=jnp.float32)
        * inv_root
    )
    row_peak = jnp.max(scores, axis=-1, keepdims=True)
    exp_scores = jnp.exp(scores - row_peak)
    attn_probs = exp_scores / jnp.sum(exp_scores, axis=-1, keepdims=True)
    probs_low = attn_probs.astype(jnp.bfloat16)
    attended = (
        jnp.einsum("hts,shd->thd", probs_low, value_heads, preferred_element_type=jnp.float32)
        .reshape(tokens_here, A)
        .astype(jnp.bfloat16)
    )
    hidden = residual.astype(jnp.float32) + jnp.dot(
        attended, full_out, preferred_element_type=jnp.float32
    )
    inv_rms = lax.rsqrt(jnp.mean(hidden * hidden, axis=-1, keepdims=True) + epsilon)
    unit_rows = hidden * inv_rms
    normed = (unit_rows * norm_gain).astype(jnp.bfloat16)
    send_buffer = jnp.dot(placing, normed).reshape(buckets)
    grad_returned, returned, features_all = run_experts(
        sizes, 1, send_buffer, grad_gathered, attended.T, gate_weight, up_weight, down_weight
    )
    expert_back = contract_first(placing, returned.reshape(experts * capacity, D))
    layer_out = (hidden + expert_back.astype(jnp.float32)).astype(jnp.bfloat16)
    grad_normed = contract_first(placing, grad_returned.reshape(experts * capacity, D))
    scaled = grad_normed * norm_gain
    resid_grad = (
        out_grad.astype(jnp.float32)
        + inv_rms * (scaled - unit_rows * jnp.mean(scaled * unit_rows, axis=-1, keepdims=True))
    ).astype(jnp.bfloat16)
    ways = data_ways * sections
    width = D // ways
    columns = resid_grad.reshape(tokens_here, ways, width).transpose(1, 0, 2)
    grad_attended = contract_last(resid_grad, full_out).astype(jnp.bfloat16)
    grad_heads = grad_attended.reshape(tokens_here, HEADS, HEAD)
    grad_probs = jnp.einsum(
        "thd,shd->hts", grad_heads, value_heads, preferred_element_type=jnp.float32
    )
    row_delta = jnp.sum(attn_probs * grad_probs, axis=-1, keepdims=True)
    grad_scores = (attn_probs * (grad_probs - row_delta)).astype(jnp.bfloat16)
    query_grad = (
        (
            jnp.einsum("hts,shd->thd", grad_scores, key_heads, preferred_element_type=jnp.float32)
            * inv_root
        )
        .reshape(tokens_here, A)
        .astype(jnp.bfloat16)
    )
    key_part = (
        jnp.einsum("hts,thd->shd", grad_scores, query_heads, preferred_element_type=jnp.float32)
        * inv_root
    )
    value_part = jnp.einsum(
        "hts,thd->shd", probs_low, grad_heads, preferred_element_type=jnp.float32
    )
    pair_parts = jnp.stack(
        [
            key_part.reshape(data_ways, tokens_here, A),
            value_part.reshape(data_ways, tokens_here, A),
        ],
        axis=1,
    ).astype(jnp.bfloat16)
    pair = (2, tokens_here, A)
    block = (weight_rows, width)
    key_value, weight_parts = call(
        closing_kernel,
        sizes,
        2,
        4 * outer + experts + 4 * ways,
        (
            pair_parts,
            features_all.reshape(ways, experts, weight_rows, tokens_here),
            columns,
        ),
        (pair, (ways,) + block),
        (
            (outer,) + pair,
            (max(outer - 1, 1),) + pair,
            columns.shape,
            (experts,) + block,
            (experts - 1,) + block,
        ),
        extra=(pltpu.SemaphoreType.DMA,),
    )
    key_grad, value_grad = key_value[0], key_value[1]
    weight_grad = weight_parts.transpose(1, 0, 2).reshape(weight_rows, D).astype(jnp.float32)
    return (layer_out, resid_grad, query_grad, key_grad, value_grad, weight_grad)


def solution(mesh):
    return jax.shard_map(
        shards,
        mesh=mesh,
        in_specs=(
            P(("section", "expert", "dp"), None),
            P(("section", "expert", "dp"), None),
            P(("section", "expert", "dp"), None),
            P(("section", "expert", "dp"), None),
            P("expert", None),
            P(),
            P("expert", None, "dp"),
            P("expert", None, "dp"),
            P("expert", "dp", None),
            P(("section", "expert", "dp"), None),
            P(("section", "expert", "dp"), None),
        ),
        out_specs=(
            P(("section", "expert", "dp"), None),
            P(("section", "expert", "dp"), None),
            P(("section", "expert", "dp"), None),
            P(("section", "expert", "dp"), None),
            P(("section", "expert", "dp"), None),
            P("expert", None),
        ),
        check_vma=False,
    )
```
